512 devices in a mesh: slab: 128 (over y, z, core), col: 4 (over x).
Axes of the slice: x: 4, y: 8, z: 8, core: 2. Of those that a mesh axis runs over, the one named last changes fastest.
Arguments:
- wave_amplitudes: float32 [128, 512, 128], P('slab', 'col'), may hold values from -6 to 6
- energy_block_per_segment: float32 [128, 512, 512], P('slab', 'col'), as said below
- tunnel_coupling_block: float32 [128, 512, 512], P('slab', 'col'), may hold values from -0.25 to 0.25
- reduced_block_reciprocal: float32 [128, 2, 512, 512], P('slab', None, 'col'), may hold values from -0.1875 to 0.1875
- beneath_reduce_multiplier: float32 [128, 2, 512, 512], P('slab', None, 'col'), may hold values from -0.09375 to 0.09375
- above_reduce_multiplier: float32 [128, 2, 512, 512], P('slab', None, 'col'), may hold values from -0.09375 to 0.09375
- beneath_solve_multiplier: float32 [128, 2, 512, 512], P('slab', None, 'col'), may hold values from -0.09375 to 0.09375
- above_solve_multiplier: float32 [128, 2, 512, 512], P('slab', None, 'col'), may hold values from -0.09375 to 0.09375
Outputs:
- psi_next: float32 [128, 512, 128], P('slab', 'col')
The draws below stay inside these ranges and needn't reach their ends.
Inputs may be any that keep to these rules, and one draw needn't show every extreme that they name: energy_block_per_segment[s] is a symmetric matrix for every slab s.
All inputs are finite; a program needn't handle non-finite values.
Results may differ from the reference program's by a relative error of at most 0.00011.
Values sent between devices are 32-bit elements; how exact they have to be, the bound alone decides.
A program may use at most 64 MiB of HBM per device.

```python
import jax
import jax.numpy as jnp
from jax import lax

BASIS_FUNCTIONS = 512
STATES = 64
SEGMENT_NUMBER = 128
LEVELS = 7


def draw_energy_block_per_segment(key, part):
    raw = jax.random.normal(key, (SEGMENT_NUMBER, BASIS_FUNCTIONS, BASIS_FUNCTIONS), jnp.float32)
    return (raw + jnp.swapaxes(raw, 1, 2)) * 0.5 ** 0.5 * BASIS_FUNCTIONS ** (-0.5)


def level_of(rng, shape, split, smallest, high):
    def one(dim, blocks):
        draws = jax.random.uniform(jax.random.fold_in(jax.random.fold_in(rng, 6), dim), (blocks,), jnp.float32, smallest / len(split), high / len(split))
        return jnp.repeat(jnp.exp(draws), shape[dim] // blocks).reshape((-1,) + (1,) * (len(shape) - dim - 1))

    factor_of = one(*split[0])
    for cut in split[1:]:
        factor_of = factor_of * one(*cut)
    return factor_of


def noise(rng, dims, scale, limit, split=(), kind=jnp.bfloat16):
    level = level_of(rng, dims, split, -0.22, 0.18) if split else 1.0
    values = jax.random.normal(rng, dims, jnp.float32) * scale * level
    return jnp.minimum(jnp.maximum(values, -limit), limit).astype(kind)


def setup_inputs(seed: int = 0) -> dict:
    streams_of = jax.random.split(jax.random.key(seed), 9)
    wave_amplitudes = noise(streams_of[0], (SEGMENT_NUMBER, BASIS_FUNCTIONS, 2 * STATES), 1.0, 6.0, ((0, 128), (1, 4)), jnp.float32)
    energy_block_per_segment = draw_energy_block_per_segment(jax.random.fold_in(streams_of[8], 71), 0)
    tunnel_coupling_block = noise(streams_of[2], (SEGMENT_NUMBER, BASIS_FUNCTIONS, BASIS_FUNCTIONS), BASIS_FUNCTIONS ** -0.5, 0.25, ((0, 128), (1, 4)), jnp.float32)
    reduced_block_reciprocal = noise(streams_of[3], (SEGMENT_NUMBER, 2, BASIS_FUNCTIONS, BASIS_FUNCTIONS), (2 * BASIS_FUNCTIONS) ** -0.5, 0.1875, ((0, 128), (2, 4)), jnp.float32)
    beneath_reduce_multiplier = noise(streams_of[4], (SEGMENT_NUMBER, 2, BASIS_FUNCTIONS, BASIS_FUNCTIONS), (8 * BASIS_FUNCTIONS) ** -0.5, 0.09375, ((0, 128), (2, 4)), jnp.float32)
    above_reduce_multiplier = noise(streams_of[5], (SEGMENT_NUMBER, 2, BASIS_FUNCTIONS, BASIS_FUNCTIONS), (8 * BASIS_FUNCTIONS) ** -0.5, 0.09375, ((0, 128), (2, 4)), jnp.float32)
    beneath_solve_multiplier = noise(streams_of[6], (SEGMENT_NUMBER, 2, BASIS_FUNCTIONS, BASIS_FUNCTIONS), (8 * BASIS_FUNCTIONS) ** -0.5, 0.09375, ((0, 128), (2, 4)), jnp.float32)
    above_solve_multiplier = noise(streams_of[7], (SEGMENT_NUMBER, 2, BASIS_FUNCTIONS, BASIS_FUNCTIONS), (8 * BASIS_FUNCTIONS) ** -0.5, 0.09375, ((0, 128), (2, 4)), jnp.float32)
    return {"wave_amplitudes": wave_amplitudes, "energy_block_per_segment": energy_block_per_segment, "tunnel_coupling_block": tunnel_coupling_block, "reduced_block_reciprocal": reduced_block_reciprocal, "beneath_reduce_multiplier": beneath_reduce_multiplier, "above_reduce_multiplier": above_reduce_multiplier, "beneath_solve_multiplier": beneath_solve_multiplier, "above_solve_multiplier": above_solve_multiplier}


half_step = 0.5
highest = lax.Precision.HIGHEST


def rotate(values):
    column = lax.broadcasted_iota(jnp.int32, values.shape, values.ndim - 1)
    return jnp.where(column % 2 == 0, -jnp.roll(values, -1, axis=-1), jnp.roll(values, 1, axis=-1))


def real_product(blocks, vectors):
    return jnp.einsum("smn,snk->smk", blocks, vectors, precision=highest)


def stacked_product_of_matrices(blocks, vectors):
    real_part = jnp.einsum("smn,snk->smk", blocks[:, 0], vectors, precision=highest)
    imag_part = jnp.einsum("smn,snk->smk", blocks[:, 1], vectors, precision=highest)
    return real_part + rotate(imag_part)


def reference(wave_amplitudes, energy_block_per_segment, tunnel_coupling_block, reduced_block_reciprocal, beneath_reduce_multiplier, above_reduce_multiplier, beneath_solve_multiplier, above_solve_multiplier):
    zero_slab = jnp.zeros_like(wave_amplitudes[:1])
    next_slab = jnp.concatenate([wave_amplitudes[1:], zero_slab], 0)
    prev_all = jnp.einsum("snm,snk->smk", tunnel_coupling_block, wave_amplitudes, precision=highest)
    prev_term = jnp.concatenate([zero_slab, prev_all[:-1]], 0)
    ham_psi = real_product(energy_block_per_segment, wave_amplitudes) + real_product(tunnel_coupling_block, next_slab) + prev_term
    reduced = wave_amplitudes - half_step * rotate(ham_psi)
    pivot_part = jnp.zeros_like(wave_amplitudes)
    for level_id in range(LEVELS):
        tier_spacing = 2 ** level_id
        present_tier = reduced[tier_spacing::2 * tier_spacing]
        pivot_piece = stacked_product_of_matrices(reduced_block_reciprocal[tier_spacing::2 * tier_spacing], present_tier)
        pivot_part = pivot_part.at[tier_spacing::2 * tier_spacing].set(pivot_piece)
        heading_beneath = stacked_product_of_matrices(beneath_reduce_multiplier[tier_spacing::2 * tier_spacing], present_tier)
        heading_above = stacked_product_of_matrices(above_reduce_multiplier[tier_spacing::2 * tier_spacing], present_tier)
        reduced = reduced.at[0::2 * tier_spacing].add(-heading_beneath)
        reduced = reduced.at[2 * tier_spacing::2 * tier_spacing].add(-heading_above[:-1])
    pivot_part = pivot_part.at[0].set(stacked_product_of_matrices(reduced_block_reciprocal[:1], reduced[:1])[0])
    solved = jnp.zeros_like(wave_amplitudes).at[0].set(pivot_part[0])
    for level_id in reversed(range(LEVELS)):
        tier_spacing = 2 ** level_id
        from_lower = solved[0::2 * tier_spacing]
        from_upper = jnp.concatenate([solved[2 * tier_spacing::2 * tier_spacing], zero_slab], 0)
        settled = pivot_part[tier_spacing::2 * tier_spacing] - stacked_product_of_matrices(beneath_solve_multiplier[tier_spacing::2 * tier_spacing], from_lower) - stacked_product_of_matrices(above_solve_multiplier[tier_spacing::2 * tier_spacing], from_upper)
        solved = solved.at[tier_spacing::2 * tier_spacing].set(settled)
    return solved
```

```python
import functools

import jax
import jax.numpy as jnp
from jax import lax
from jax.experimental import pallas as pl
from jax.experimental.pallas import tpu as pltpu
from jax.sharding import PartitionSpec as P

MESH = pl.DeviceIdType.MESH
half_step = 0.5


def rotate(values):
    width = values.shape[-1]
    column = lax.broadcasted_iota(jnp.int32, values.shape, values.ndim - 1)
    return jnp.where(
        column % 2 == 0,
        -pltpu.roll(values, width - 1, values.ndim - 1),
        pltpu.roll(values, 1, values.ndim - 1),
    )


def split(values):
    high = values.astype(jnp.bfloat16)
    low = (values - high.astype(jnp.float32)).astype(jnp.bfloat16)
    return high, low


def split_wide(values):
    return jnp.concatenate(split(values), axis=1)


def three_pass(tall_pair, wide_pair):
    product = jnp.dot(tall_pair, wide_pair, preferred_element_type=jnp.float32)
    rows, columns = product.shape[0] // 2, product.shape[1] // 2
    return product[:rows, :columns] + (product[:rows, columns:] + product[rows:, :columns])


def complex_rows(tall_pair, wide_pair):
    both = three_pass(tall_pair, wide_pair)
    rows = both.shape[0] // 2
    return both[:rows] + rotate(both[rows:])


def kernel(
    slabs,
    levels,
    parts,
    psi_h,
    energy_h,
    tunnel_h,
    pivot_h,
    beneath_reduce_h,
    above_reduce_h,
    beneath_solve_h,
    above_solve_h,
    out,
    psi_full,
    next_full,
    prev_parts,
    prev_send,
    energy_v,
    tunnel_v,
    blocks_v,
    energy_w,
    tunnel_w,
    pivot_w,
    reduce_w,
    solve_w,
    x_full,
    pivot_part,
    reduce_in,
    reduce_out,
    solve_in,
    load_sem,
    psi_send,
    psi_recv,
    next_send,
    next_recv,
    prev_send_sem,
    prev_recv,
    x_send,
    x_recv,
    reduce_send,
    reduce_recv,
    solve_send,
    solve_recv,
):
    s = lax.axis_index("slab")
    c = lax.axis_index("col")
    level = jnp.int32(0)
    reach = jnp.int32(1)
    for k in range(1, levels + 1):
        at_least = s % (2**k) == 0
        level = jnp.where(at_least, k, level)
        reach = jnp.where(at_least, 2**k, reach)
    is_root = s == 0
    partner_levels = jnp.minimum(level + 1, levels)
    rows = psi_h.shape[1]
    depth = parts * rows

    def everyone_of(slab, act):
        for step in (2, 1, 3, 0):
            act((slab, (c + step) % parts))

    def rest_of_row(act):
        for step in (2, 1, 3):
            act((s, (c + step) % parts))

    def load(index, source, target):
        return pltpu.make_async_copy(source, target, load_sem.at[index])

    loads = [
        load(0, psi_h.at[0], psi_full.at[c]),
        load(1, tunnel_h.at[0], tunnel_v),
        load(2, energy_h.at[0], energy_v),
        load(3, beneath_reduce_h.at[0], blocks_v.at[0]),
        load(4, above_reduce_h.at[0], blocks_v.at[1]),
        load(5, pivot_h.at[0], blocks_v.at[2]),
        load(6, beneath_solve_h.at[0], blocks_v.at[3]),
        load(7, above_solve_h.at[0], blocks_v.at[4]),
    ]
    for copy in loads:
        copy.start()

    barrier = pltpu.get_barrier_semaphore()

    def greet(device):
        pl.semaphore_signal(barrier, inc=1, device_id=device, device_id_type=MESH)

    rest_of_row(greet)

    @pl.loop(0, partner_levels)
    def _(j):
        distance = jnp.left_shift(jnp.int32(1), j)

        @pl.when(s - distance >= 0)
        def _():
            everyone_of(s - distance, greet)

        @pl.when(s + distance < slabs)
        def _():
            everyone_of(s + distance, greet)

    has_above = s + reach < slabs
    both_sides = jnp.where(is_root, levels, 2 * level + 1 + has_above.astype(jnp.int32))

    loads[0].wait()
    loads[1].wait()
    own = psi_full[c]
    tunnel = tunnel_v[...]
    prev_send[...] = three_pass(
        jnp.concatenate(split(tunnel.T), axis=0), split_wide(own)
    ).reshape(prev_send.shape)
    tunnel_w[...] = jnp.concatenate(split(tunnel), axis=0)

    pl.semaphore_wait(barrier, (parts - 1) + parts * both_sides)

    def remote(source, target, send, recv, device):
        return pltpu.make_async_remote_copy(
            src_ref=source, dst_ref=target, send_sem=send, recv_sem=recv,
            device_id=device, device_id_type=MESH,
        )

    def send_psi_row():
        rest_of_row(
            lambda device: remote(
                psi_full.at[c], psi_full.at[c], psi_send, psi_recv, device
            ).start()
        )

    def send_next():
        @pl.when(s > 0)
        def _():
            everyone_of(
                s - 1,
                lambda device: remote(
                    psi_full.at[c], next_full.at[c], next_send, next_recv, device
                ).start(),
            )

    def send_prev():
        @pl.when(s + 1 < slabs)
        def _():
            everyone_of(
                s + 1,
                lambda device: remote(
                    prev_send.at[device[1]], prev_parts.at[c], prev_send_sem, prev_recv, device
                ).start(),
            )

    @pl.when(s % 2 == 1)
    def _():
        send_psi_row()
        send_next()
        send_prev()

    @pl.when(s % 2 == 0)
    def _():
        send_next()
        send_prev()
        send_psi_row()

    def stacked(index):
        block = blocks_v[index].reshape(2 * rows, depth)
        return jnp.concatenate(split(block), axis=0)

    loads[2].wait()
    energy_w[...] = jnp.concatenate(split(energy_v[...]), axis=0)
    loads[3].wait()
    reduce_w[0] = stacked(0)
    loads[4].wait()
    reduce_w[1] = stacked(1)

    def arrived(ref, sem):
        pltpu.make_async_copy(ref, ref, sem).wait()

    arrived(psi_full.at[pl.ds(0, parts - 1)], psi_recv)
    x_full[c] = three_pass(energy_w[...], split_wide(psi_full[...].reshape(depth, -1)))

    @pl.when(s + 1 < slabs)
    def _():
        arrived(next_full, next_recv)
        x_full[c] += three_pass(tunnel_w[...], split_wide(next_full[...].reshape(depth, -1)))

    @pl.when(s > 0)
    def _():
        arrived(prev_parts, prev_recv)
        x_full[c] += (prev_parts[0] + prev_parts[1]) + (prev_parts[2] + prev_parts[3])

    x_full[c] = psi_full[c] - half_step * rotate(x_full[c])
    rest_of_row(
        lambda device: remote(x_full.at[c], x_full.at[c], x_send, x_recv, device).start()
    )

    loads[5].wait()
    pivot_w[...] = stacked(2)
    loads[6].wait()
    solve_w[0] = stacked(3)
    loads[7].wait()
    solve_w[1] = stacked(4)

    arrived(x_full.at[pl.ds(0, parts - 1)], x_recv)
    arrived(x_full.at[pl.ds(0, parts - 1)], x_send)

    @pl.loop(0, level)
    def _(j):
        arrived(reduce_in.at[j, 1], reduce_recv.at[j, 1])
        x_full[...] -= reduce_in[j, 1]

        @pl.when(s > 0)
        def _():
            arrived(reduce_in.at[j, 0], reduce_recv.at[j, 0])
            x_full[...] -= reduce_in[j, 0]

    wide = split_wide(x_full[...].reshape(depth, -1))
    odd_pair = (s // reach // 2) % 2

    @pl.when(s > 0)
    def _():
        @pl.loop(0, 2)
        def _(turn):
            side = jnp.where(odd_pair == 1, turn, 1 - turn)
            target = s + (2 * side - 1) * reach

            @pl.when(target < slabs)
            def _():
                reduce_out[side] = complex_rows(reduce_w[side], wide)
                everyone_of(
                    target,
                    lambda device: remote(
                        reduce_out.at[side],
                        reduce_in.at[level, 1 - side, c],
                        reduce_send.at[side],
                        reduce_recv.at[level, 1 - side],
                        device,
                    ).start(),
                )

    pivot_part[...] = complex_rows(pivot_w[...], wide)

    @pl.when(s > 0)
    def _():
        @pl.loop(0, 2)
        def _(turn):
            side = jnp.where(odd_pair == 1, 1 - turn, turn)

            @pl.when(s + (2 * side - 1) * reach < slabs)
            def _():
                arrived(solve_in.at[side], solve_recv.at[side])
                pivot_part[...] -= complex_rows(
                    solve_w[side], split_wide(solve_in[side].reshape(depth, -1))
                )

    def send_solved(j, side):
        target = s + (2 * side - 1) * jnp.left_shift(jnp.int32(1), j)
        everyone_of(
            target,
            lambda device: remote(
                pivot_part,
                solve_in.at[1 - side, c],
                solve_send.at[j, side],
                solve_recv.at[1 - side],
                device,
            ).start(),
        )

    @pl.loop(0, level)
    def _(i):
        j = level - 1 - i
        send_solved(j, 1)

        @pl.when(s > 0)
        def _():
            send_solved(j, 0)

    out[0] = pivot_part[...]

    arrived(psi_full.at[pl.ds(0, parts - 1)], psi_send)

    @pl.when(s > 0)
    def _():
        arrived(next_full, next_send)

    @pl.when(s + 1 < slabs)
    def _():
        arrived(prev_parts, prev_send_sem)

    @pl.when(s > 0)
    def _():
        @pl.loop(0, 2)
        def _(side):
            @pl.when(s + (2 * side - 1) * reach < slabs)
            def _():
                arrived(solve_in.at[side], reduce_send.at[side])

    @pl.loop(0, level)
    def _(j):
        arrived(solve_in.at[1], solve_send.at[j, 1])

        @pl.when(s > 0)
        def _():
            arrived(solve_in.at[0], solve_send.at[j, 0])


def per_device(*args):
    slabs = lax.axis_size("slab")
    levels = slabs.bit_length() - 1
    parts = lax.axis_size("col")
    psi = args[0]
    rows, width = psi.shape[1:]
    depth = parts * rows
    f32, bf16 = jnp.float32, jnp.bfloat16
    gathered = pltpu.VMEM((parts, rows, width), f32)
    dma = pltpu.SemaphoreType.DMA
    return pl.pallas_call(
        functools.partial(kernel, slabs, levels, parts),
        out_shape=jax.ShapeDtypeStruct(psi.shape, psi.dtype),
        in_specs=[pl.BlockSpec(memory_space=pl.ANY)] * len(args),
        out_specs=pl.BlockSpec(memory_space=pltpu.VMEM),
        scratch_shapes=[
            gathered,
            gathered,
            gathered,
            gathered,
            pltpu.VMEM((rows, depth), f32),
            pltpu.VMEM((rows, depth), f32),
            pltpu.VMEM((5, 2, rows, depth), f32),
            pltpu.VMEM((2 * rows, depth), bf16),
            pltpu.VMEM((2 * rows, depth), bf16),
            pltpu.VMEM((4 * rows, depth), bf16),
            pltpu.VMEM((2, 4 * rows, depth), bf16),
            pltpu.VMEM((2, 4 * rows, depth), bf16),
            gathered,
            pltpu.VMEM((rows, width), f32),
            pltpu.VMEM((levels, 2, parts, rows, width), f32),
            pltpu.VMEM((2, rows, width), f32),
            pltpu.VMEM((2, parts, rows, width), f32),
            dma((8,)),
            dma,
            dma,
            dma,
            dma,
            dma,
            dma,
            dma,
            dma,
            dma((2,)),
            dma((levels, 2)),
            dma((levels, 2)),
            dma((2,)),
        ],
        compiler_params=pltpu.CompilerParams(
            collective_id=0, has_side_effects=True, vmem_limit_bytes=40 * 2**20
        ),
    )(*args)


def solution(mesh):
    vector = P("slab", "col", None)
    block = P("slab", None, "col", None)
    return jax.shard_map(
        per_device,
        mesh=mesh,
        in_specs=(vector,) * 3 + (block,) * 5,
        out_specs=vector,
        check_vma=False,
    )
```

```python
import functools

import jax
import jax.numpy as jnp
from jax import lax
from jax.experimental import pallas as pl
from jax.experimental.pallas import tpu as pltpu
from jax.sharding import PartitionSpec as P

MESH = pl.DeviceIdType.MESH
half_step = 0.5


def rotate(values):
    width = values.shape[-1]
    column = lax.broadcasted_iota(jnp.int32, values.shape, values.ndim - 1)
    return jnp.where(
        column % 2 == 0,
        -pltpu.roll(values, width - 1, values.ndim - 1),
        pltpu.roll(values, 1, values.ndim - 1),
    )


def split(values):
    high = values.astype(jnp.bfloat16)
    low = (values - high.astype(jnp.float32)).astype(jnp.bfloat16)
    return high, low


def split_wide(values):
    return jnp.concatenate(split(values), axis=1)


def three_pass(tall_pair, wide_pair):
    product = jnp.dot(tall_pair, wide_pair, preferred_element_type=jnp.float32)
    rows, columns = product.shape[0] // 2, product.shape[1] // 2
    return product[:rows, :columns] + (product[:rows, columns:] + product[rows:, :columns])


def complex_rows(tall_pair, wide_pair):
    both = three_pass(tall_pair, wide_pair)
    rows = both.shape[0] // 2
    return both[:rows] + rotate(both[rows:])


def kernel(
    slabs,
    levels,
    parts,
    psi_h,
    energy_h,
    tunnel_h,
    pivot_h,
    beneath_reduce_h,
    above_reduce_h,
    beneath_solve_h,
    above_solve_h,
    out,
    psi_full,
    next_full,
    prev_parts,
    prev_send,
    energy_v,
    tunnel_v,
    blocks_v,
    energy_w,
    tunnel_w,
    pivot_w,
    reduce_w,
    solve_w,
    x_full,
    pivot_part,
    reduce_in,
    reduce_out,
    solve_in,
    load_sem,
    psi_send,
    psi_recv,
    next_send,
    next_recv,
    prev_send_sem,
    prev_recv,
    x_send,
    x_recv,
    reduce_send,
    reduce_recv,
    solve_send,
    solve_recv,
):
    s = lax.axis_index("slab")
    c = lax.axis_index("col")
    level = jnp.int32(0)
    reach = jnp.int32(1)
    for k in range(1, levels + 1):
        at_least = s % (2**k) == 0
        level = jnp.where(at_least, k, level)
        reach = jnp.where(at_least, 2**k, reach)
    is_root = s == 0
    partner_levels = jnp.minimum(level + 1, levels)
    rows = psi_h.shape[1]
    depth = parts * rows

    def everyone_of(slab, act):
        for step in (2, 1, 3, 0):
            act((slab, (c + step) % parts))

    def rest_of_row(act):
        for step in (2, 1, 3):
            act((s, (c + step) % parts))

    def load(index, source, target):
        return pltpu.make_async_copy(source, target, load_sem.at[index])

    loads = [
        load(0, psi_h.at[0], psi_full.at[c]),
        load(1, tunnel_h.at[0], tunnel_v),
        load(2, energy_h.at[0], energy_v),
        load(3, beneath_reduce_h.at[0], blocks_v.at[0]),
        load(4, above_reduce_h.at[0], blocks_v.at[1]),
        load(5, pivot_h.at[0], blocks_v.at[2]),
        load(6, beneath_solve_h.at[0], blocks_v.at[3]),
        load(7, above_solve_h.at[0], blocks_v.at[4]),
    ]
    for copy in loads:
        copy.start()

    barrier = pltpu.get_barrier_semaphore()

    def greet(device):
        pl.semaphore_signal(barrier, inc=1, device_id=device, device_id_type=MESH)

    rest_of_row(greet)

    @pl.loop(0, partner_levels)
    def _(j):
        distance = jnp.left_shift(jnp.int32(1), j)

        @pl.when(s - distance >= 0)
        def _():
            everyone_of(s - distance, greet)

        @pl.when(s + distance < slabs)
        def _():
            everyone_of(s + distance, greet)

    has_above = s + reach < slabs
    both_sides = jnp.where(is_root, levels, 2 * level + 1 + has_above.astype(jnp.int32))

    loads[0].wait()
    loads[1].wait()
    own = psi_full[c]
    tunnel = tunnel_v[...]
    prev_send[...] = three_pass(
        jnp.concatenate(split(tunnel.T), axis=0), split_wide(own)
    ).reshape(prev_send.shape)
    tunnel_w[...] = jnp.concatenate(split(tunnel), axis=0)

    pl.semaphore_wait(barrier, (parts - 1) + parts * both_sides)

    def remote(source, target, send, recv, device):
        return pltpu.make_async_remote_copy(
            src_ref=source, dst_ref=target, send_sem=send, recv_sem=recv,
            device_id=device, device_id_type=MESH,
        )

    def send_psi_row():
        rest_of_row(
            lambda device: remote(
                psi_full.at[c], psi_full.at[c], psi_send, psi_recv, device
            ).start()
        )

    def send_next():
        @pl.when(s > 0)
        def _():
            everyone_of(
                s - 1,
                lambda device: remote(
                    psi_full.at[c], next_full.at[c], next_send, next_recv, device
                ).start(),
            )

    def send_prev():
        @pl.when(s + 1 < slabs)
        def _():
            everyone_of(
                s + 1,
                lambda device: remote(
                    prev_send.at[device[1]], prev_parts.at[c], prev_send_sem, prev_recv, device
                ).start(),
            )

    odd = s % 2 == 1

    @pl.when(odd)
    def _():
        send_psi_row()

    @pl.when(jnp.logical_not(odd))
    def _():
        send_next()
        send_prev()
        send_psi_row()

    def stacked(index):
        block = blocks_v[index].reshape(2 * rows, depth)
        return jnp.concatenate(split(block), axis=0)

    loads[2].wait()
    energy_w[...] = jnp.concatenate(split(energy_v[...]), axis=0)
    loads[3].wait()
    reduce_w[0] = stacked(0)
    loads[4].wait()
    reduce_w[1] = stacked(1)

    def arrived(ref, sem):
        pltpu.make_async_copy(ref, ref, sem).wait()

    arrived(psi_full.at[pl.ds(0, parts - 1)], psi_recv)
    x_full[c] = three_pass(energy_w[...], split_wide(psi_full[...].reshape(depth, -1)))

    @pl.when(s + 1 < slabs)
    def _():
        arrived(next_full, next_recv)
        x_full[c] += three_pass(tunnel_w[...], split_wide(next_full[...].reshape(depth, -1)))

    @pl.when(s > 0)
    def _():
        arrived(prev_parts, prev_recv)
        x_full[c] += (prev_parts[0] + prev_parts[1]) + (prev_parts[2] + prev_parts[3])

    x_full[c] = psi_full[c] - half_step * rotate(x_full[c])
    rest_of_row(
        lambda device: remote(x_full.at[c], x_full.at[c], x_send, x_recv, device).start()
    )

    @pl.when(odd)
    def _():
        remote(psi_full, next_full, next_send, next_recv, (s - 1, c)).start()
        send_prev()

    loads[5].wait()
    pivot_w[...] = stacked(2)
    loads[6].wait()
    solve_w[0] = stacked(3)
    loads[7].wait()
    solve_w[1] = stacked(4)

    arrived(x_full.at[pl.ds(0, parts - 1)], x_recv)
    arrived(x_full.at[pl.ds(0, parts - 1)], x_send)

    @pl.loop(0, level)
    def _(j):
        arrived(reduce_in.at[j, 1], reduce_recv.at[j, 1])
        x_full[...] -= reduce_in[j, 1]

        @pl.when(s > 0)
        def _():
            arrived(reduce_in.at[j, 0], reduce_recv.at[j, 0])
            x_full[...] -= reduce_in[j, 0]

    wide = split_wide(x_full[...].reshape(depth, -1))
    odd_pair = (s // reach // 2) % 2

    @pl.when(s > 0)
    def _():
        @pl.loop(0, 2)
        def _(turn):
            side = jnp.where(odd_pair == 1, turn, 1 - turn)
            target = s + (2 * side - 1) * reach

            @pl.when(target < slabs)
            def _():
                reduce_out[side] = complex_rows(reduce_w[side], wide)
                everyone_of(
                    target,
                    lambda device: remote(
                        reduce_out.at[side],
                        reduce_in.at[level, 1 - side, c],
                        reduce_send.at[side],
                        reduce_recv.at[level, 1 - side],
                        device,
                    ).start(),
                )

    pivot_part[...] = complex_rows(pivot_w[...], wide)

    @pl.when(s > 0)
    def _():
        @pl.loop(0, 2)
        def _(turn):
            side = jnp.where(odd_pair == 1, 1 - turn, turn)

            @pl.when(s + (2 * side - 1) * reach < slabs)
            def _():
                arrived(solve_in.at[side], solve_recv.at[side])
                pivot_part[...] -= complex_rows(
                    solve_w[side], split_wide(solve_in[side].reshape(depth, -1))
                )

    def send_solved(j, side):
        target = s + (2 * side - 1) * jnp.left_shift(jnp.int32(1), j)
        everyone_of(
            target,
            lambda device: remote(
                pivot_part,
                solve_in.at[1 - side, c],
                solve_send.at[j, side],
                solve_recv.at[1 - side],
                device,
            ).start(),
        )

    @pl.loop(0, level)
    def _(i):
        j = level - 1 - i
        send_solved(j, 1)

        @pl.when(s > 0)
        def _():
            send_solved(j, 0)

    out[0] = pivot_part[...]

    arrived(psi_full.at[pl.ds(0, parts - 1)], psi_send)

    @pl.when(s > 0)
    def _():
        arrived(next_full, next_send)

    @pl.when(s + 1 < slabs)
    def _():
        arrived(prev_parts, prev_send_sem)

    @pl.when(s > 0)
    def _():
        @pl.loop(0, 2)
        def _(side):
            @pl.when(s + (2 * side - 1) * reach < slabs)
            def _():
                arrived(solve_in.at[side], reduce_send.at[side])

    @pl.loop(0, level)
    def _(j):
        arrived(solve_in.at[1], solve_send.at[j, 1])

        @pl.when(s > 0)
        def _():
            arrived(solve_in.at[0], solve_send.at[j, 0])


def per_device(*args):
    slabs = lax.axis_size("slab")
    levels = slabs.bit_length() - 1
    parts = lax.axis_size("col")
    psi = args[0]
    rows, width = psi.shape[1:]
    depth = parts * rows
    f32, bf16 = jnp.float32, jnp.bfloat16
    gathered = pltpu.VMEM((parts, rows, width), f32)
    dma = pltpu.SemaphoreType.DMA
    return pl.pallas_call(
        functools.partial(kernel, slabs, levels, parts),
        out_shape=jax.ShapeDtypeStruct(psi.shape, psi.dtype),
        in_specs=[pl.BlockSpec(memory_space=pltpu.HBM)] * len(args),
        out_specs=pl.BlockSpec(memory_space=pltpu.VMEM),
        scratch_shapes=[
            gathered,
            gathered,
            gathered,
            gathered,
            pltpu.VMEM((rows, depth), f32),
            pltpu.VMEM((rows, depth), f32),
            pltpu.VMEM((5, 2, rows, depth), f32),
            pltpu.VMEM((2 * rows, depth), bf16),
            pltpu.VMEM((2 * rows, depth), bf16),
            pltpu.VMEM((4 * rows, depth), bf16),
            pltpu.VMEM((2, 4 * rows, depth), bf16),
            pltpu.VMEM((2, 4 * rows, depth), bf16),
            gathered,
            pltpu.VMEM((rows, width), f32),
            pltpu.VMEM((levels, 2, parts, rows, width), f32),
            pltpu.VMEM((2, rows, width), f32),
            pltpu.VMEM((2, parts, rows, width), f32),
            dma((8,)),
            dma,
            dma,
            dma,
            dma,
            dma,
            dma,
            dma,
            dma,
            dma((2,)),
            dma((levels, 2)),
            dma((levels, 2)),
            dma((2,)),
        ],
        compiler_params=pltpu.CompilerParams(
            collective_id=0, has_side_effects=True, vmem_limit_bytes=40 * 2**20
        ),
    )(*args)


def solution(mesh):
    vector = P("slab", "col", None)
    block = P("slab", None, "col", None)
    return jax.shard_map(
        per_device,
        mesh=mesh,
        in_specs=(vector,) * 3 + (block,) * 5,
        out_specs=vector,
        check_vma=False,
    )
```

```python
import functools

import jax
import jax.numpy as jnp
from jax import lax
from jax.experimental import pallas as pl
from jax.experimental.pallas import tpu as pltpu
from jax.sharding import PartitionSpec as P

MESH = pl.DeviceIdType.MESH
half_step = 0.5


def rotate(values):
    width = values.shape[-1]
    column = lax.broadcasted_iota(jnp.int32, values.shape, values.ndim - 1)
    return jnp.where(
        column % 2 == 0,
        -pltpu.roll(values, width - 1, values.ndim - 1),
        pltpu.roll(values, 1, values.ndim - 1),
    )


def split(values):
    high = values.astype(jnp.bfloat16)
    low = (values - high.astype(jnp.float32)).astype(jnp.bfloat16)
    return high, low


def split_wide(values):
    return jnp.concatenate(split(values), axis=1)


def three_pass(tall_pair, wide_pair):
    product = jnp.dot(tall_pair, wide_pair, preferred_element_type=jnp.float32)
    rows, columns = product.shape[0] // 2, product.shape[1] // 2
    return product[:rows, :columns] + (product[:rows, columns:] + product[rows:, :columns])


def complex_rows(tall_pair, wide_pair):
    both = three_pass(tall_pair, wide_pair)
    rows = both.shape[0] // 2
    return both[:rows] + rotate(both[rows:])


def kernel(
    slabs,
    levels,
    parts,
    psi_h,
    energy_h,
    tunnel_h,
    pivot_h,
    beneath_reduce_h,
    above_reduce_h,
    beneath_solve_h,
    above_solve_h,
    out,
    psi_full,
    next_full,
    prev_parts,
    prev_send,
    energy_v,
    tunnel_v,
    blocks_v,
    energy_w,
    tunnel_w,
    pivot_w,
    reduce_w,
    solve_w,
    x_full,
    pivot_part,
    reduce_in,
    reduce_out,
    solve_in,
    load_sem,
    psi_send,
    psi_recv,
    next_send,
    next_recv,
    prev_send_sem,
    prev_recv,
    x_send,
    x_recv,
    reduce_send,
    reduce_recv,
    solve_send,
    solve_recv,
):
    s = lax.axis_index("slab")
    c = lax.axis_index("col")
    level = jnp.int32(0)
    reach = jnp.int32(1)
    for k in range(1, levels + 1):
        at_least = s % (2**k) == 0
        level = jnp.where(at_least, k, level)
        reach = jnp.where(at_least, 2**k, reach)
    is_root = s == 0
    partner_levels = jnp.minimum(level + 1, levels)
    rows = psi_h.shape[1]
    depth = parts * rows

    def everyone_of(slab, act):
        for step in (2, 1, 3, 0):
            act((slab, (c + step) % parts))

    def rest_of_row(act):
        for step in (2, 1, 3):
            act((s, (c + step) % parts))

    def load(index, source, target):
        return pltpu.make_async_copy(source, target, load_sem.at[index])

    loads = [
        load(0, psi_h.at[0], psi_full.at[c]),
        load(1, tunnel_h.at[0], tunnel_v),
        load(2, energy_h.at[0], energy_v),
        load(3, beneath_reduce_h.at[0], blocks_v.at[0]),
        load(4, above_reduce_h.at[0], blocks_v.at[1]),
        load(5, pivot_h.at[0], blocks_v.at[2]),
        load(6, beneath_solve_h.at[0], blocks_v.at[3]),
        load(7, above_solve_h.at[0], blocks_v.at[4]),
    ]
    for copy in loads:
        copy.start()

    barrier = pltpu.get_barrier_semaphore()

    def greet(device):
        pl.semaphore_signal(barrier, inc=1, device_id=device, device_id_type=MESH)

    rest_of_row(greet)

    @pl.loop(0, partner_levels)
    def _(j):
        distance = jnp.left_shift(jnp.int32(1), j)

        @pl.when(s - distance >= 0)
        def _():
            everyone_of(s - distance, greet)

        @pl.when(s + distance < slabs)
        def _():
            everyone_of(s + distance, greet)

    has_above = s + reach < slabs
    both_sides = jnp.where(is_root, levels, 2 * level + 1 + has_above.astype(jnp.int32))

    loads[0].wait()
    loads[1].wait()
    own = psi_full[c]
    tunnel = tunnel_v[...]
    prev_send[...] = three_pass(
        jnp.concatenate(split(tunnel.T), axis=0), split_wide(own)
    ).reshape(prev_send.shape)
    tunnel_w[...] = jnp.concatenate(split(tunnel), axis=0)

    pl.semaphore_wait(barrier, (parts - 1) + parts * both_sides)

    def remote(source, target, send, recv, device):
        return pltpu.make_async_remote_copy(
            src_ref=source, dst_ref=target, send_sem=send, recv_sem=recv,
            device_id=device, device_id_type=MESH,
        )

    def send_psi_row():
        rest_of_row(
            lambda device: remote(
                psi_full.at[c], psi_full.at[c], psi_send, psi_recv, device
            ).start()
        )

    def send_next():
        @pl.when(s > 0)
        def _():
            everyone_of(
                s - 1,
                lambda device: remote(
                    psi_full.at[c], next_full.at[c], next_send, next_recv, device
                ).start(),
            )

    def send_prev():
        @pl.when(s + 1 < slabs)
        def _():
            everyone_of(
                s + 1,
                lambda device: remote(
                    prev_send.at[device[1]], prev_parts.at[c], prev_send_sem, prev_recv, device
                ).start(),
            )

    odd = s % 2 == 1

    @pl.when(odd)
    def _():
        send_psi_row()

    @pl.when(jnp.logical_not(odd))
    def _():
        send_next()
        send_prev()
        send_psi_row()

    def stacked(index):
        block = blocks_v[index].reshape(2 * rows, depth)
        return jnp.concatenate(split(block), axis=0)

    loads[2].wait()
    energy_w[...] = jnp.concatenate(split(energy_v[...]), axis=0)
    loads[3].wait()
    reduce_w[0] = stacked(0)
    loads[4].wait()
    reduce_w[1] = stacked(1)

    def arrived(ref, sem):
        pltpu.make_async_copy(ref, ref, sem).wait()

    arrived(psi_full.at[pl.ds(0, parts - 1)], psi_recv)
    x_full[c] = three_pass(energy_w[...], split_wide(psi_full[...].reshape(depth, -1)))

    @pl.when(s + 1 < slabs)
    def _():
        arrived(next_full, next_recv)
        x_full[c] += three_pass(tunnel_w[...], split_wide(next_full[...].reshape(depth, -1)))

    @pl.when(s > 0)
    def _():
        arrived(prev_parts, prev_recv)
        x_full[c] += (prev_parts[0] + prev_parts[1]) + (prev_parts[2] + prev_parts[3])

    x_full[c] = psi_full[c] - half_step * rotate(x_full[c])
    rest_of_row(
        lambda device: remote(x_full.at[c], x_full.at[c], x_send, x_recv, device).start()
    )

    @pl.when(odd)
    def _():
        remote(psi_full, next_full, next_send, next_recv, (s - 1, c)).start()
        send_prev()

    loads[5].wait()
    pivot_w[...] = stacked(2)
    loads[6].wait()
    solve_w[0] = stacked(3)
    loads[7].wait()
    solve_w[1] = stacked(4)

    arrived(x_full.at[pl.ds(0, parts - 1)], x_recv)
    arrived(x_full.at[pl.ds(0, parts - 1)], x_send)

    @pl.loop(0, level)
    def _(j):
        arrived(reduce_in.at[j, 1], reduce_recv.at[j, 1])
        x_full[...] -= reduce_in[j, 1]

        @pl.when(s > 0)
        def _():
            arrived(reduce_in.at[j, 0], reduce_recv.at[j, 0])
            x_full[...] -= reduce_in[j, 0]

    wide = split_wide(x_full[...].reshape(depth, -1))
    odd_pair = (s // reach // 2) % 2

    @pl.when(s > 0)
    def _():
        @pl.loop(0, 2)
        def _(turn):
            side = jnp.where(odd_pair == 1, turn, 1 - turn)
            target = s + (2 * side - 1) * reach

            @pl.when(target < slabs)
            def _():
                reduce_out[side] = complex_rows(reduce_w[side], wide)
                everyone_of(
                    target,
                    lambda device: remote(
                        reduce_out.at[side],
                        reduce_in.at[level, 1 - side, c],
                        reduce_send.at[side],
                        reduce_recv.at[level, 1 - side],
                        device,
                    ).start(),
                )

    pivot_part[...] = complex_rows(pivot_w[...], wide)

    @pl.when(s > 0)
    def _():
        @pl.loop(0, 2)
        def _(turn):
            side = jnp.where(odd_pair == 1, 1 - turn, turn)

            @pl.when(s + (2 * side - 1) * reach < slabs)
            def _():
                arrived(solve_in.at[side], solve_recv.at[side])
                pivot_part[...] -= complex_rows(
                    solve_w[side], split_wide(solve_in[side].reshape(depth, -1))
                )

    def send_solved(j, side):
        target = s + (2 * side - 1) * jnp.left_shift(jnp.int32(1), j)
        everyone_of(
            target,
            lambda device: remote(
                pivot_part,
                solve_in.at[1 - side, c],
                solve_send.at[j, side],
                solve_recv.at[1 - side],
                device,
            ).start(),
        )

    @pl.loop(0, level)
    def _(i):
        j = level - 1 - i
        send_solved(j, 1)

        @pl.when(s > 0)
        def _():
            send_solved(j, 0)

    out[0] = pivot_part[...]

    arrived(psi_full.at[pl.ds(0, parts - 1)], psi_send)

    @pl.when(s > 0)
    def _():
        arrived(next_full, next_send)

    @pl.when(s + 1 < slabs)
    def _():
        arrived(prev_parts, prev_send_sem)

    @pl.when(s > 0)
    def _():
        @pl.loop(0, 2)
        def _(side):
            @pl.when(s + (2 * side - 1) * reach < slabs)
            def _():
                arrived(solve_in.at[side], reduce_send.at[side])

    @pl.loop(0, level)
    def _(j):
        arrived(solve_in.at[1], solve_send.at[j, 1])

        @pl.when(s > 0)
        def _():
            arrived(solve_in.at[0], solve_send.at[j, 0])


def per_device(*args):
    slabs = lax.axis_size("slab")
    levels = slabs.bit_length() - 1
    parts = lax.axis_size("col")
    psi = args[0]
    rows, width = psi.shape[1:]
    depth = parts * rows
    f32, bf16 = jnp.float32, jnp.bfloat16
    gathered = pltpu.VMEM((parts, rows, width), f32)
    dma = pltpu.SemaphoreType.DMA
    return pl.pallas_call(
        functools.partial(kernel, slabs, levels, parts),
        out_shape=jax.ShapeDtypeStruct(psi.shape, psi.dtype),
        in_specs=[pl.BlockSpec(memory_space=pltpu.HBM)] * len(args),
        out_specs=pl.BlockSpec(memory_space=pltpu.VMEM),
        scratch_shapes=[
            gathered,
            gathered,
            gathered,
            gathered,
            pltpu.VMEM((rows, depth), f32),
            pltpu.VMEM((rows, depth), f32),
            pltpu.VMEM((5, 2, rows, depth), f32),
            pltpu.VMEM((2 * rows, depth), bf16),
            pltpu.VMEM((2 * rows, depth), bf16),
            pltpu.VMEM((4 * rows, depth), bf16),
            pltpu.VMEM((2, 4 * rows, depth), bf16),
            pltpu.VMEM((2, 4 * rows, depth), bf16),
            gathered,
            pltpu.VMEM((rows, width), f32),
            pltpu.VMEM((levels, 2, parts, rows, width), f32),
            pltpu.VMEM((2, rows, width), f32),
            pltpu.VMEM((2, parts, rows, width), f32),
            dma((8,)),
            dma,
            dma,
            dma,
            dma,
            dma,
            dma,
            dma,
            dma,
            dma((2,)),
            dma((levels, 2)),
            dma((levels, 2)),
            dma((2,)),
        ],
        compiler_params=pltpu.CompilerParams(
            collective_id=0, has_side_effects=True, vmem_limit_bytes=56 * 2**20
        ),
    )(*args)


def solution(mesh):
    vector = P("slab", "col", None)
    block = P("slab", None, "col", None)
    return jax.shard_map(
        per_device,
        mesh=mesh,
        in_specs=(vector,) * 3 + (block,) * 5,
        out_specs=vector,
        check_vma=False,
    )
```

```python
import functools

import jax
import jax.numpy as jnp
from jax import lax
from jax.experimental import pallas as pl
from jax.experimental.pallas import tpu as pltpu
from jax.sharding import PartitionSpec as P

MESH = pl.DeviceIdType.MESH
half_step = 0.5
ROW_LEVELS = 2
BENEATH_R, ABOVE_R, PIVOT, BENEATH_S, ABOVE_S = range(5)


def rotate(values):
    height = values.shape[0]
    row = lax.broadcasted_iota(jnp.int32, values.shape, 0)
    return jnp.where(
        row % 2 == 0, -pltpu.roll(values, height - 1, 0), pltpu.roll(values, 1, 0)
    )


def split(values):
    high = values.astype(jnp.bfloat16)
    low = (values - high.astype(jnp.float32)).astype(jnp.bfloat16)
    return high, low


def split_tall(values):
    return jnp.concatenate(split(values), axis=0)


def fold(product):
    m, n = product.shape[0] // 2, product.shape[1] // 2
    return product[:m, :n] + (product[m:, :n] + product[:m, n:])


def times_rows(tall, block_rows):
    return fold(
        lax.dot_general(
            tall, block_rows, (((1,), (1,)), ((), ())), preferred_element_type=jnp.float32
        )
    )


def times_columns(tall, block_columns):
    return fold(jnp.dot(tall, block_columns, preferred_element_type=jnp.float32))


def join(both):
    n = both.shape[1] // 2
    return both[:, :n] + rotate(both[:, n:])


def side_by_side(pieces):
    return jnp.concatenate([pieces[k] for k in range(pieces.shape[0])], axis=1)


def place_of(slab, levels):
    level, reach = jnp.int32(0), jnp.int32(1)
    for k in range(1, levels + 1):
        at_least = slab % (2**k) == 0
        level = jnp.where(at_least, k, level)
        reach = jnp.where(at_least, 2**k, reach)
    return level, reach


def kernel(slabs, levels, parts, *refs):
    (
        psi_h, energy_h, tunnel_h, pivot_h, beneath_reduce_h, above_reduce_h,
        beneath_solve_h, above_solve_h, out,
        psi_raw, energy_v, tunnel_v, blocks_v, turned_v,
        psi_full, next_full, prev_parts, prev_send_v, x_full,
        energy_w, tunnel_w, own_w, row_raw, row_w, state_raw, state_w,
        pivot_odd, odd_out,
        rhs_row, row_in, row_x, row_out,
        rhs_state, state_in, state_x, state_out,
        solve_in, solved, odd_in, out_in,
        load_sem, psi_send, psi_recv, next_send, next_recv, prev_send, prev_recv,
        x_send, x_recv, rhs_send, rhs_recv, mat_send, mat_recv, odd_send, up_send,
        reduce_recv, solve_send, solve_recv, last_send, last_recv, out_send, out_recv, go,
    ) = refs
    s = lax.axis_index("slab")
    c = lax.axis_index("col")
    odd = s % 2 == 1
    even = s % 2 == 0
    chip = s // 2
    e = chip * 2
    level, reach = place_of(e, levels)
    level_next, _ = place_of(e + 2, levels)
    is_root = e == 0
    not_root = e > 0
    state_role = level > ROW_LEVELS
    row_role = level <= ROW_LEVELS
    has_next = e + 2 < slabs
    rows, width = psi_h.shape[1:]
    depth = parts * rows
    quarter = width // parts

    def around(slab, act, skip_own=False):
        for step in (2, 1, 3) if skip_own else (2, 1, 3, 0):
            act((slab, (c + step) % parts))

    def arrived(ref, sem):
        pltpu.make_async_copy(ref, ref, sem).wait()

    def send(source, target, send_sem, recv_sem, device):
        pltpu.make_async_remote_copy(
            src_ref=source, dst_ref=target, send_sem=send_sem, recv_sem=recv_sem,
            device_id=device, device_id_type=MESH,
        ).start()

    def states_of(col):
        return pl.ds(pl.multiple_of(col * quarter, quarter), quarter)

    def load(index, source, target):
        return pltpu.make_async_copy(source, target, load_sem.at[index])

    loads = [
        load(0, psi_h.at[0], psi_raw),
        load(1, tunnel_h.at[0], tunnel_v),
        load(2, energy_h.at[0], energy_v),
        load(3, beneath_reduce_h.at[0], blocks_v.at[BENEATH_R]),
        load(4, above_reduce_h.at[0], blocks_v.at[ABOVE_R]),
        load(5, pivot_h.at[0], blocks_v.at[PIVOT]),
        load(6, beneath_solve_h.at[0], blocks_v.at[BENEATH_S]),
        load(7, above_solve_h.at[0], blocks_v.at[ABOVE_S]),
    ]
    for copy in loads:
        copy.start()

    barrier = pltpu.get_barrier_semaphore()

    def greet(device):
        pl.semaphore_signal(barrier, inc=1, device_id=device, device_id_type=MESH)

    around(s, greet, skip_own=True)
    around(s + 1 - 2 * (s % 2), greet)
    expected = jnp.int32(2 * parts - 1)

    @pl.when(jnp.logical_and(even, not_root))
    def _():
        around(s - 1, greet)

    @pl.when(jnp.logical_and(odd, has_next))
    def _():
        around(s + 1, greet)

    expected += parts * jnp.where(odd, has_next, not_root).astype(jnp.int32)
    for j in range(1, levels):
        for sign in (-1, 1):
            target = s + sign * 2**j
            there = jnp.logical_and(target >= 0, target < slabs)
            if j > 1:
                there = jnp.logical_and(there, j <= level)
            there = jnp.logical_and(there, odd)
            count = parts if j <= max(ROW_LEVELS, 1) else 1
            expected += count * there.astype(jnp.int32)

            @pl.when(there)
            def _():
                if count > 1:
                    around(target, greet)
                else:
                    greet((target, c))

    loads[0].wait()
    loads[1].wait()
    own = psi_raw[...].T
    psi_full[c] = own
    tunnel = tunnel_v[...]
    wide_tunnel = jnp.concatenate(split(tunnel), axis=1)
    partial = times_columns(split_tall(own), wide_tunnel)
    for k in range(parts):
        prev_send_v[k] = partial[:, k * rows : (k + 1) * rows]

    pl.semaphore_wait(barrier, expected)

    def send_psi_row():
        around(
            s,
            lambda device: send(psi_full.at[c], psi_full.at[c], psi_send, psi_recv, device),
            skip_own=True,
        )

    def send_prev():
        around(
            s + 1,
            lambda device: send(
                prev_send_v.at[device[1]], prev_parts.at[c], prev_send, prev_recv, device
            ),
        )

    @pl.when(odd)
    def _():
        send_psi_row()

    @pl.when(even)
    def _():
        @pl.when(not_root)
        def _():
            around(
                s - 1,
                lambda device: send(
                    psi_full.at[c], next_full.at[c], next_send, next_recv, device
                ),
            )

        send_prev()
        send_psi_row()

    def stacked(block):
        return split_tall(block.reshape(2 * rows, depth))

    tunnel_w[...] = split_tall(tunnel)
    loads[2].wait()
    energy_w[...] = split_tall(energy_v[...])
    for index in range(5):
        loads[3 + index].wait()

    def turn(index):
        for part in range(2):
            turned_v[index, part] = blocks_v[index, part].T

    def pass_on(index):
        around(
            s + 1,
            lambda device: send(
                turned_v.at[index],
                state_raw.at[index, c],
                mat_send.at[index],
                mat_recv.at[index],
                device,
            ),
        )

    @pl.when(even)
    def _():
        @pl.when(row_role)
        def _():
            for index in (BENEATH_R, ABOVE_R):
                send(
                    blocks_v.at[index], row_raw.at[index], mat_send.at[index],
                    mat_recv.at[index], (s + 1, c),
                )

        @pl.when(jnp.logical_and(state_role, not_root))
        def _():
            for index in (BENEATH_R, ABOVE_R):
                turn(index)
                pass_on(index)

    @pl.when(odd)
    def _():
        own_w[BENEATH_R] = stacked(blocks_v[BENEATH_R])
        own_w[ABOVE_R] = stacked(blocks_v[ABOVE_R])

    arrived(psi_full.at[pl.ds(0, parts - 1)], psi_recv)
    x_full[c] = times_rows(split_tall(side_by_side(psi_full[...])), energy_w[...])

    @pl.when(s > 0)
    def _():
        arrived(prev_parts, prev_recv)
        x_full[c] += (prev_parts[0] + prev_parts[1]) + (prev_parts[2] + prev_parts[3])

    @pl.when(s + 1 < slabs)
    def _():
        arrived(next_full, next_recv)
        x_full[c] += times_rows(split_tall(side_by_side(next_full[...])), tunnel_w[...])

    x_full[c] = psi_full[c] - half_step * rotate(x_full[c])

    @pl.when(even)
    def _():
        @pl.when(state_role)
        def _():
            around(
                s + 1,
                lambda device: send(
                    x_full.at[c, states_of(device[1])], rhs_state.at[c], rhs_send, rhs_recv, device
                ),
            )

        @pl.when(row_role)
        def _():
            around(
                s + 1,
                lambda device: send(x_full.at[c], rhs_row.at[c], rhs_send, rhs_recv, device),
            )

        turn(PIVOT)

        @pl.when(not_root)
        def _():
            turn(BENEATH_S)
            turn(ABOVE_S)

        pl.semaphore_wait(go, 1)
        pass_on(PIVOT)

        @pl.when(not_root)
        def _():
            pass_on(BENEATH_S)
            pass_on(ABOVE_S)

        arrived(out_in, out_recv)
        out[0] = out_in[...].T

        arrived(psi_full.at[pl.ds(0, parts - 1)], psi_send)
        arrived(prev_parts, prev_send)

        @pl.when(not_root)
        def _():
            arrived(next_full, next_send)
            arrived(state_raw.at[BENEATH_S], mat_send.at[BENEATH_S])
            arrived(state_raw.at[ABOVE_S], mat_send.at[ABOVE_S])

            @pl.when(state_role)
            def _():
                arrived(state_raw.at[BENEATH_R], mat_send.at[BENEATH_R])
                arrived(state_raw.at[ABOVE_R], mat_send.at[ABOVE_R])

        arrived(state_raw.at[PIVOT], mat_send.at[PIVOT])

        @pl.when(state_role)
        def _():
            arrived(rhs_state, rhs_send)

        @pl.when(row_role)
        def _():
            arrived(rhs_row, rhs_send)
            arrived(row_raw.at[BENEATH_R], mat_send.at[BENEATH_R])
            arrived(row_raw.at[ABOVE_R], mat_send.at[ABOVE_R])

    @pl.when(odd)
    def _():
        around(
            s,
            lambda device: send(x_full.at[c], x_full.at[c], x_send, x_recv, device),
            skip_own=True,
        )
        send(psi_full, next_full, next_send, next_recv, (s - 1, c))

        @pl.when(has_next)
        def _():
            send_prev()

        own_w[PIVOT] = stacked(blocks_v[PIVOT])
        own_w[BENEATH_S] = stacked(blocks_v[BENEATH_S])
        own_w[ABOVE_S] = stacked(blocks_v[ABOVE_S])

        arrived(x_full.at[pl.ds(0, parts - 1)], x_recv)
        tall = split_tall(side_by_side(x_full[...]))

        def send_rows(source, host, to_state, tier, side, sem, skip_own=False):
            @pl.when(to_state)
            def _():
                around(
                    host,
                    lambda device: send(
                        source.at[states_of(device[1])],
                        state_in.at[tier, side, c],
                        sem,
                        reduce_recv.at[tier, side],
                        device,
                    ),
                    skip_own,
                )

            @pl.when(jnp.logical_not(to_state))
            def _():
                around(
                    host,
                    lambda device: send(
                        source,
                        row_in.at[jnp.minimum(tier, ROW_LEVELS - 1), side, c],
                        sem,
                        reduce_recv.at[tier, side],
                        device,
                    ),
                    skip_own,
                )

        def odd_beneath():
            odd_out[0] = join(times_rows(tall, own_w[BENEATH_R]))
            send_rows(odd_out.at[0], s, state_role, 0, 1, odd_send.at[0], skip_own=True)

            @pl.when(state_role)
            def _():
                state_in[0, 1, c] = odd_out[0, states_of(c)]

            @pl.when(row_role)
            def _():
                row_in[0, 1, c] = odd_out[0]

        def odd_above():
            @pl.when(has_next)
            def _():
                odd_out[1] = join(times_rows(tall, own_w[ABOVE_R]))
                send_rows(
                    odd_out.at[1], s + 2, level_next > ROW_LEVELS, 0, 0, odd_send.at[1]
                )

        @pl.when(chip % 2 == 1)
        def _():
            odd_beneath()
            odd_above()

        @pl.when(chip % 2 == 0)
        def _():
            odd_above()
            odd_beneath()

        def let_go():
            pl.semaphore_signal(go, inc=1, device_id=(s - 1, c), device_id_type=MESH)

        @pl.when(state_role)
        def _():
            let_go()

        pivot_odd[...] = join(times_rows(tall, own_w[PIVOT]))

        odd_pair = (e // reach // 2) % 2

        def convert(index):
            arrived(state_raw.at[index], mat_recv.at[index])
            for part in range(2):
                for k in range(parts):
                    at = (part * parts + k) * rows
                    high, low = split(state_raw[index, k, part])
                    state_w[index, :, at : at + rows] = high
                    state_w[index, :, 2 * depth + at : 2 * depth + at + rows] = low

        def state_product(index, pieces):
            return join(times_columns(split_tall(side_by_side(pieces)), state_w[index]))

        @pl.when(state_role)
        def _():
            @pl.when(not_root)
            def _():
                @pl.loop(0, 2)
                def _(index):
                    convert(index)

            arrived(rhs_state, rhs_recv)
            arrived(state_in.at[0, 1, pl.ds(0, parts - 1)], reduce_recv.at[0, 1])
            state_x[...] = rhs_state[...] - state_in[0, 1]

            @pl.when(not_root)
            def _():
                arrived(state_in.at[0, 0], reduce_recv.at[0, 0])
                state_x[...] -= state_in[0, 0]

            @pl.loop(1, level)
            def _(j):
                arrived(state_in.at[j, 1], reduce_recv.at[j, 1])
                state_x[...] -= state_in[j, 1]

                @pl.when(not_root)
                def _():
                    arrived(state_in.at[j, 0], reduce_recv.at[j, 0])
                    state_x[...] -= state_in[j, 0]

            @pl.when(not_root)
            def _():
                @pl.loop(0, 2)
                def _(turn_id):
                    side = jnp.where(odd_pair == 1, turn_id, 1 - turn_id)
                    target = e + (2 * side - 1) * reach

                    @pl.when(target < slabs)
                    def _():
                        product = state_product(side, state_x[...])
                        for k in range(parts):
                            state_out[side, k] = product[:, k * rows : (k + 1) * rows]
                        send(
                            state_out.at[side],
                            state_in.at[level, 1 - side],
                            up_send.at[side],
                            reduce_recv.at[level, 1 - side],
                            (target + 1, c),
                        )

        @pl.when(row_role)
        def _():
            for index in (BENEATH_R, ABOVE_R):
                arrived(row_raw.at[index], mat_recv.at[index])
                row_w[index] = stacked(row_raw[index])
            arrived(rhs_row, rhs_recv)
            arrived(row_in.at[0, 1, pl.ds(0, parts - 1)], reduce_recv.at[0, 1])
            arrived(row_in.at[0, 0], reduce_recv.at[0, 0])
            row_x[...] = rhs_row[...] - row_in[0, 1] - row_in[0, 0]

            for j in range(1, ROW_LEVELS):
                @pl.when(level > j)
                def _():
                    arrived(row_in.at[j, 1], reduce_recv.at[j, 1])
                    arrived(row_in.at[j, 0], reduce_recv.at[j, 0])
                    row_x[...] -= row_in[j, 1] + row_in[j, 0]

            row_tall = split_tall(side_by_side(row_x[...]))

            @pl.loop(0, 2)
            def _(turn_id):
                side = jnp.where(odd_pair == 1, turn_id, 1 - turn_id)
                target = e + (2 * side - 1) * reach

                @pl.when(target < slabs)
                def _():
                    row_out[side] = join(times_rows(row_tall, row_w[side]))
                    target_level, _ = place_of(target, levels)
                    send_rows(
                        row_out.at[side],
                        target + 1,
                        target_level > ROW_LEVELS,
                        level,
                        1 - side,
                        up_send.at[side],
                    )

            let_go()
            state_x[...] = row_x[:, states_of(c)]

        convert(PIVOT)
        product = state_product(PIVOT, state_x[...])
        for k in range(parts):
            solved[k] = product[:, k * rows : (k + 1) * rows]

        @pl.when(not_root)
        def _():
            @pl.loop(BENEATH_S, ABOVE_S + 1)
            def _(index):
                convert(index)

            @pl.loop(0, 2)
            def _(turn_id):
                side = jnp.where(odd_pair == 1, 1 - turn_id, turn_id)

                @pl.when(e + (2 * side - 1) * reach < slabs)
                def _():
                    arrived(solve_in.at[side], solve_recv.at[side])
                    product = state_product(BENEATH_S + side, solve_in[side])
                    for k in range(parts):
                        solved[k] -= product[:, k * rows : (k + 1) * rows]

        def send_solved(j, side):
            target = s + (2 * side - 1) * jnp.left_shift(jnp.int32(1), j)
            send(
                solved, solve_in.at[1 - side], solve_send.at[j, side],
                solve_recv.at[1 - side], (target, c),
            )

        @pl.loop(0, level - 1)
        def _(i):
            j = level - 1 - i
            send_solved(j, 1)

            @pl.when(not_root)
            def _():
                send_solved(j, 0)

        @pl.when(not_root)
        def _():
            around(
                s - 2,
                lambda device: send(
                    solved, odd_in.at[1, :, states_of(c)], last_send.at[1], last_recv.at[1], device
                ),
            )

        around(
            s,
            lambda device: send(
                solved, odd_in.at[0, :, states_of(c)], last_send.at[0], last_recv.at[0], device
            ),
            skip_own=True,
        )
        odd_in[0, :, states_of(c)] = solved[...]
        around(
            s - 1,
            lambda device: send(
                solved.at[device[1]], out_in.at[states_of(c)], out_send, out_recv, device
            ),
        )

        def settle(side):
            def take():
                if side == 0:
                    arrived(solved_three, last_recv.at[0])
                else:
                    arrived(odd_in.at[1], last_recv.at[1])
                pivot_odd[...] -= join(
                    times_rows(split_tall(side_by_side(odd_in[side])), own_w[BENEATH_S + side])
                )

            if side == 0:
                take()
            else:
                pl.when(has_next)(take)

        solved_three = psi_full.at[pl.ds(0, parts - 1)]

        @pl.when(chip % 2 == 1)
        def _():
            settle(1)
            settle(0)

        @pl.when(chip % 2 == 0)
        def _():
            settle(0)
            settle(1)

        out[0] = pivot_odd[...].T

        arrived(psi_full.at[pl.ds(0, parts - 1)], psi_send)
        arrived(x_full.at[pl.ds(0, parts - 1)], x_send)
        arrived(next_full, next_send)

        @pl.when(state_role)
        def _():
            arrived(rhs_state.at[pl.ds(0, parts - 1)], odd_send.at[0])

        @pl.when(row_role)
        def _():
            arrived(rhs_row.at[pl.ds(0, parts - 1)], odd_send.at[0])

        @pl.when(has_next)
        def _():
            arrived(prev_parts, prev_send)

            @pl.when(level_next > ROW_LEVELS)
            def _():
                arrived(rhs_state, odd_send.at[1])

            @pl.when(level_next <= ROW_LEVELS)
            def _():
                arrived(rhs_row, odd_send.at[1])

        @pl.when(not_root)
        def _():
            @pl.loop(0, 2)
            def _(side):
                target = e + (2 * side - 1) * reach
                target_level, _ = place_of(target, levels)

                @pl.when(target < slabs)
                def _():
                    small = target_level > ROW_LEVELS

                    @pl.when(small)
                    def _():
                        arrived(rhs_state, up_send.at[side])

                    @pl.when(jnp.logical_not(small))
                    def _():
                        arrived(rhs_row, up_send.at[side])

            arrived(rhs_row, last_send.at[1])

        arrived(psi_full.at[pl.ds(0, parts - 1)], last_send.at[0])
        arrived(rhs_state, out_send)

        @pl.loop(1, level)
        def _(j):
            arrived(solved, solve_send.at[j, 1])

            @pl.when(not_root)
            def _():
                arrived(solved, solve_send.at[j, 0])


def per_device(*args):
    slabs = lax.axis_size("slab")
    levels = slabs.bit_length() - 1
    parts = lax.axis_size("col")
    psi = args[0]
    rows, width = psi.shape[1:]
    depth = parts * rows
    quarter = width // parts
    f32, bf16 = jnp.float32, jnp.bfloat16

    def whole(*lead):
        return pltpu.VMEM((*lead, parts, width, rows), f32)

    def piece(*lead):
        return pltpu.VMEM((*lead, parts, quarter, rows), f32)

    dma = pltpu.SemaphoreType.DMA
    return pl.pallas_call(
        functools.partial(kernel, slabs, levels, parts),
        out_shape=jax.ShapeDtypeStruct(psi.shape, psi.dtype),
        in_specs=[pl.BlockSpec(memory_space=pl.ANY)] * len(args),
        out_specs=pl.BlockSpec(memory_space=pltpu.VMEM),
        scratch_shapes=[
            pltpu.VMEM((rows, width), f32),
            pltpu.VMEM((rows, depth), f32),
            pltpu.VMEM((rows, depth), f32),
            pltpu.VMEM((5, 2, rows, depth), f32),
            pltpu.VMEM((5, 2, depth, rows), f32),
            whole(),
            whole(),
            whole(),
            whole(),
            whole(),
            pltpu.VMEM((2 * rows, depth), bf16),
            pltpu.VMEM((2 * rows, depth), bf16),
            pltpu.VMEM((5, 4 * rows, depth), bf16),
            pltpu.VMEM((2, 2, rows, depth), f32),
            pltpu.VMEM((2, 4 * rows, depth), bf16),
            pltpu.VMEM((5, parts, 2, depth, rows), f32),
            pltpu.VMEM((5, depth, 4 * depth), bf16),
            pltpu.VMEM((width, rows), f32),
            pltpu.VMEM((2, width, rows), f32),
            whole(),
            whole(ROW_LEVELS, 2),
            whole(),
            pltpu.VMEM((2, width, rows), f32),
            piece(),
            piece(levels, 2),
            piece(),
            piece(2),
            piece(2),
            piece(),
            whole(2),
            pltpu.VMEM((width, rows), f32),
            dma((8,)),
            *[dma] * 10,
            dma((5,)),
            dma((5,)),
            dma((2,)),
            dma((2,)),
            dma((levels, 2)),
            dma((levels, 2)),
            dma((2,)),
            dma((2,)),
            dma((2,)),
            dma,
            dma,
            pltpu.SemaphoreType.REGULAR,
        ],
        compiler_params=pltpu.CompilerParams(
            collective_id=0, has_side_effects=True, vmem_limit_bytes=56 * 2**20
        ),
    )(*args)


def solution(mesh):
    vector = P("slab", "col", None)
    block = P("slab", None, "col", None)
    return jax.shard_map(
        per_device,
        mesh=mesh,
        in_specs=(vector,) * 3 + (block,) * 5,
        out_specs=vector,
        check_vma=False,
    )
```

```python
import functools

import jax
import jax.numpy as jnp
from jax import lax
from jax.experimental import pallas as pl
from jax.experimental.pallas import tpu as pltpu
from jax.sharding import PartitionSpec as P

MESH = pl.DeviceIdType.MESH
half_step = 0.5
ROW_LEVELS = 2
BENEATH_R, ABOVE_R, PIVOT, BENEATH_S, ABOVE_S = range(5)


def rotate(values):
    height = values.shape[0]
    row = lax.broadcasted_iota(jnp.int32, values.shape, 0)
    return jnp.where(
        row % 2 == 0, -pltpu.roll(values, height - 1, 0), pltpu.roll(values, 1, 0)
    )


def split(values):
    high = values.astype(jnp.bfloat16)
    low = (values - high.astype(jnp.float32)).astype(jnp.bfloat16)
    return high, low


def split_tall(values):
    return jnp.concatenate(split(values), axis=0)


def fold(product):
    m, n = product.shape[0] // 2, product.shape[1] // 2
    return product[:m, :n] + (product[m:, :n] + product[:m, n:])


def times_rows(tall, block_rows):
    return fold(
        lax.dot_general(
            tall, block_rows, (((1,), (1,)), ((), ())), preferred_element_type=jnp.float32
        )
    )


def times_columns(tall, block_columns):
    return fold(jnp.dot(tall, block_columns, preferred_element_type=jnp.float32))


def join(both):
    n = both.shape[1] // 2
    return both[:, :n] + rotate(both[:, n:])


def side_by_side(pieces):
    return jnp.concatenate([pieces[k] for k in range(pieces.shape[0])], axis=1)


def place_of(slab, levels):
    level, reach = jnp.int32(0), jnp.int32(1)
    for k in range(1, levels + 1):
        at_least = slab % (2**k) == 0
        level = jnp.where(at_least, k, level)
        reach = jnp.where(at_least, 2**k, reach)
    return level, reach


def kernel(slabs, levels, parts, *refs):
    (
        psi_h, energy_h, tunnel_h, pivot_h, beneath_reduce_h, above_reduce_h,
        beneath_solve_h, above_solve_h, out,
        psi_raw, energy_v, tunnel_v, blocks_v, turned_v,
        psi_full, next_full, prev_parts, prev_send_v, x_full,
        energy_w, tunnel_w, own_w, row_raw, row_w, state_raw, state_w,
        pivot_odd, odd_out,
        rhs_row, row_in, row_x, row_out,
        rhs_state, state_in, state_x, state_out,
        solve_in, solved, odd_in, out_in, pivot_rows,
        load_sem, psi_send, psi_recv, next_send, next_recv, prev_send, prev_recv,
        x_send, x_recv, rhs_send, rhs_recv, mat_send, mat_recv, odd_send, up_send,
        reduce_recv, solve_send, solve_recv, last_send, last_recv, out_send, out_recv,
        gather_send, gather_recv, part_send, part_recv, go,
    ) = refs
    s = lax.axis_index("slab")
    c = lax.axis_index("col")
    odd = s % 2 == 1
    even = s % 2 == 0
    chip = s // 2
    e = chip * 2
    level, reach = place_of(e, levels)
    level_next, _ = place_of(e + 2, levels)
    is_root = e == 0
    not_root = e > 0
    has_above = e + reach < slabs
    state_role = level > ROW_LEVELS
    row_role = level <= ROW_LEVELS
    has_next = e + 2 < slabs
    rows, width = psi_h.shape[1:]
    depth = parts * rows
    quarter = width // parts

    def around(slab, act, skip_own=False):
        for step in (2, 1, 3) if skip_own else (2, 1, 3, 0):
            act((slab, (c + step) % parts))

    def arrived(ref, sem):
        pltpu.make_async_copy(ref, ref, sem).wait()

    def send(source, target, send_sem, recv_sem, device):
        pltpu.make_async_remote_copy(
            src_ref=source, dst_ref=target, send_sem=send_sem, recv_sem=recv_sem,
            device_id=device, device_id_type=MESH,
        ).start()

    def states_of(col):
        return pl.ds(pl.multiple_of(col * quarter, quarter), quarter)

    def load(index, source, target):
        return pltpu.make_async_copy(source, target, load_sem.at[index])

    loads = [
        load(0, psi_h.at[0], psi_raw),
        load(1, tunnel_h.at[0], tunnel_v),
        load(2, energy_h.at[0], energy_v),
        load(3, beneath_reduce_h.at[0], blocks_v.at[BENEATH_R]),
        load(4, above_reduce_h.at[0], blocks_v.at[ABOVE_R]),
        load(5, pivot_h.at[0], blocks_v.at[PIVOT]),
        load(6, beneath_solve_h.at[0], blocks_v.at[BENEATH_S]),
        load(7, above_solve_h.at[0], blocks_v.at[ABOVE_S]),
    ]
    for copy in loads:
        copy.start()

    barrier = pltpu.get_barrier_semaphore()

    def greet(device):
        pl.semaphore_signal(barrier, inc=1, device_id=device, device_id_type=MESH)

    around(s, greet, skip_own=True)
    around(s + 1 - 2 * (s % 2), greet)
    expected = jnp.int32(2 * parts - 1)

    @pl.when(jnp.logical_and(even, not_root))
    def _():
        around(s - 1, greet)

    @pl.when(jnp.logical_and(odd, has_next))
    def _():
        around(s + 1, greet)

    expected += parts * jnp.where(odd, has_next, not_root).astype(jnp.int32)
    for j in range(1, levels):
        for sign in (-1, 1):
            target = s + sign * 2**j
            there = jnp.logical_and(target >= 0, target < slabs)
            if j > 1:
                there = jnp.logical_and(there, j <= level)
            there = jnp.logical_and(there, odd)
            count = parts if j <= max(ROW_LEVELS, 1) else 1
            expected += count * there.astype(jnp.int32)

            @pl.when(there)
            def _():
                if count > 1:
                    around(target, greet)
                else:
                    greet((target, c))

    loads[0].wait()
    loads[1].wait()
    own = psi_raw[...].T
    psi_full[c] = own
    tunnel = tunnel_v[...]
    wide_tunnel = jnp.concatenate(split(tunnel), axis=1)
    partial = times_columns(split_tall(own), wide_tunnel)
    for k in range(parts):
        prev_send_v[k] = partial[:, k * rows : (k + 1) * rows]

    pl.semaphore_wait(barrier, expected)

    def send_psi_row():
        around(
            s,
            lambda device: send(psi_full.at[c], psi_full.at[c], psi_send, psi_recv, device),
            skip_own=True,
        )

    def send_prev():
        around(
            s + 1,
            lambda device: send(
                prev_send_v.at[device[1]], prev_parts.at[c], prev_send, prev_recv, device
            ),
        )

    @pl.when(odd)
    def _():
        send_psi_row()

    @pl.when(even)
    def _():
        @pl.when(not_root)
        def _():
            around(
                s - 1,
                lambda device: send(
                    psi_full.at[c], next_full.at[c], next_send, next_recv, device
                ),
            )

        send_prev()
        send_psi_row()

    def stacked(block):
        return split_tall(block.reshape(2 * rows, depth))

    tunnel_w[...] = split_tall(tunnel)
    loads[2].wait()
    energy_w[...] = split_tall(energy_v[...])
    for index in range(5):
        loads[3 + index].wait()

    def turn(index):
        for part in range(2):
            turned_v[index, part] = blocks_v[index, part].T

    def pass_on(index):
        around(
            s + 1,
            lambda device: send(
                turned_v.at[index],
                state_raw.at[index, c],
                mat_send.at[index],
                mat_recv.at[index],
                device,
            ),
        )

    def hand_over(index):
        send(
            blocks_v.at[index], row_raw.at[index], mat_send.at[index], mat_recv.at[index],
            (s + 1, c),
        )

    @pl.when(even)
    def _():
        @pl.when(is_root)
        def _():
            turn(PIVOT)
            pass_on(PIVOT)

        @pl.when(not_root)
        def _():
            hand_over(PIVOT)

            @pl.when(row_role)
            def _():
                hand_over(BENEATH_R)
                hand_over(ABOVE_R)

            @pl.when(state_role)
            def _():
                turn(BENEATH_R)
                pass_on(BENEATH_R)

                @pl.when(has_above)
                def _():
                    turn(ABOVE_R)
                    pass_on(ABOVE_R)

    @pl.when(odd)
    def _():
        own_w[BENEATH_R] = stacked(blocks_v[BENEATH_R])
        own_w[ABOVE_R] = stacked(blocks_v[ABOVE_R])

    arrived(psi_full.at[pl.ds(0, parts - 1)], psi_recv)
    x_full[c] = times_rows(split_tall(side_by_side(psi_full[...])), energy_w[...])

    @pl.when(s > 0)
    def _():
        arrived(prev_parts, prev_recv)
        x_full[c] += (prev_parts[0] + prev_parts[1]) + (prev_parts[2] + prev_parts[3])

    @pl.when(s + 1 < slabs)
    def _():
        arrived(next_full, next_recv)
        x_full[c] += times_rows(split_tall(side_by_side(next_full[...])), tunnel_w[...])

    x_full[c] = psi_full[c] - half_step * rotate(x_full[c])

    @pl.when(even)
    def _():
        @pl.when(state_role)
        def _():
            around(
                s + 1,
                lambda device: send(
                    x_full.at[c, states_of(device[1])], rhs_state.at[c], rhs_send, rhs_recv, device
                ),
            )

        @pl.when(row_role)
        def _():
            around(
                s + 1,
                lambda device: send(x_full.at[c], rhs_row.at[c], rhs_send, rhs_recv, device),
            )

        @pl.when(not_root)
        def _():
            turn(BENEATH_S)
            turn(ABOVE_S)

        pl.semaphore_wait(go, 1)

        @pl.when(not_root)
        def _():
            pass_on(BENEATH_S)

            @pl.when(has_above)
            def _():
                pass_on(ABOVE_S)

        arrived(out_in, out_recv)
        out[0] = out_in[...].T

        arrived(psi_full.at[pl.ds(0, parts - 1)], psi_send)
        arrived(prev_parts, prev_send)

        @pl.when(not_root)
        def _():
            arrived(next_full, next_send)
            arrived(state_raw.at[BENEATH_S], mat_send.at[BENEATH_S])
            arrived(row_raw.at[PIVOT], mat_send.at[PIVOT])

            @pl.when(has_above)
            def _():
                arrived(state_raw.at[ABOVE_S], mat_send.at[ABOVE_S])

            @pl.when(state_role)
            def _():
                arrived(state_raw.at[BENEATH_R], mat_send.at[BENEATH_R])

                @pl.when(has_above)
                def _():
                    arrived(state_raw.at[ABOVE_R], mat_send.at[ABOVE_R])

            @pl.when(row_role)
            def _():
                arrived(row_raw.at[BENEATH_R], mat_send.at[BENEATH_R])
                arrived(row_raw.at[ABOVE_R], mat_send.at[ABOVE_R])

        @pl.when(is_root)
        def _():
            arrived(state_raw.at[PIVOT], mat_send.at[PIVOT])

        @pl.when(state_role)
        def _():
            arrived(rhs_state, rhs_send)

        @pl.when(row_role)
        def _():
            arrived(rhs_row, rhs_send)

    @pl.when(odd)
    def _():
        around(
            s,
            lambda device: send(x_full.at[c], x_full.at[c], x_send, x_recv, device),
            skip_own=True,
        )
        send(psi_full, next_full, next_send, next_recv, (s - 1, c))

        @pl.when(has_next)
        def _():
            send_prev()

        own_w[PIVOT] = stacked(blocks_v[PIVOT])
        own_w[BENEATH_S] = stacked(blocks_v[BENEATH_S])
        own_w[ABOVE_S] = stacked(blocks_v[ABOVE_S])

        arrived(x_full.at[pl.ds(0, parts - 1)], x_recv)
        tall = split_tall(side_by_side(x_full[...]))

        def send_rows(source, host, to_state, tier, side, sem, skip_own=False):
            @pl.when(to_state)
            def _():
                around(
                    host,
                    lambda device: send(
                        source.at[states_of(device[1])],
                        state_in.at[tier, side, c],
                        sem,
                        reduce_recv.at[tier, side],
                        device,
                    ),
                    skip_own,
                )

            @pl.when(jnp.logical_not(to_state))
            def _():
                around(
                    host,
                    lambda device: send(
                        source,
                        row_in.at[jnp.minimum(tier, ROW_LEVELS - 1), side, c],
                        sem,
                        reduce_recv.at[tier, side],
                        device,
                    ),
                    skip_own,
                )

        def odd_beneath():
            odd_out[0] = join(times_rows(tall, own_w[BENEATH_R]))
            send_rows(odd_out.at[0], s, state_role, 0, 1, odd_send.at[0], skip_own=True)

            @pl.when(state_role)
            def _():
                state_in[0, 1, c] = odd_out[0, states_of(c)]

            @pl.when(row_role)
            def _():
                row_in[0, 1, c] = odd_out[0]

        def odd_above():
            @pl.when(has_next)
            def _():
                odd_out[1] = join(times_rows(tall, own_w[ABOVE_R]))
                send_rows(
                    odd_out.at[1], s + 2, level_next > ROW_LEVELS, 0, 0, odd_send.at[1]
                )

        @pl.when(chip % 2 == 1)
        def _():
            odd_beneath()
            odd_above()

        @pl.when(chip % 2 == 0)
        def _():
            odd_above()
            odd_beneath()

        def let_go():
            pl.semaphore_signal(go, inc=1, device_id=(s - 1, c), device_id_type=MESH)

        @pl.when(state_role)
        def _():
            let_go()

        pivot_odd[...] = join(times_rows(tall, own_w[PIVOT]))

        odd_pair = (e // reach // 2) % 2

        def convert(index):
            arrived(state_raw.at[index], mat_recv.at[index])
            for part in range(2):
                for k in range(parts):
                    at = (part * parts + k) * rows
                    high, low = split(state_raw[index, k, part])
                    state_w[index, :, at : at + rows] = high
                    state_w[index, :, 2 * depth + at : 2 * depth + at + rows] = low

        def convert_pair(first):
            @pl.loop(first, first + 1 + has_above.astype(jnp.int32))
            def _(index):
                convert(index)

        def state_product(index, pieces):
            return join(times_columns(split_tall(side_by_side(pieces)), state_w[index]))

        @pl.when(state_role)
        def _():
            @pl.when(not_root)
            def _():
                convert_pair(BENEATH_R)

            arrived(rhs_state, rhs_recv)
            arrived(state_in.at[0, 1, pl.ds(0, parts - 1)], reduce_recv.at[0, 1])
            state_x[...] = rhs_state[...] - state_in[0, 1]

            @pl.when(not_root)
            def _():
                arrived(state_in.at[0, 0], reduce_recv.at[0, 0])
                state_x[...] -= state_in[0, 0]

            @pl.loop(1, level)
            def _(j):
                arrived(state_in.at[j, 1], reduce_recv.at[j, 1])
                state_x[...] -= state_in[j, 1]

                @pl.when(not_root)
                def _():
                    arrived(state_in.at[j, 0], reduce_recv.at[j, 0])
                    state_x[...] -= state_in[j, 0]

            @pl.when(not_root)
            def _():
                @pl.loop(0, 2)
                def _(turn_id):
                    side = jnp.where(odd_pair == 1, turn_id, 1 - turn_id)
                    target = e + (2 * side - 1) * reach

                    @pl.when(target < slabs)
                    def _():
                        product = state_product(side, state_x[...])
                        for k in range(parts):
                            state_out[side, k] = product[:, k * rows : (k + 1) * rows]
                        send(
                            state_out.at[side],
                            state_in.at[level, 1 - side],
                            up_send.at[side],
                            reduce_recv.at[level, 1 - side],
                            (target + 1, c),
                        )

        @pl.when(row_role)
        def _():
            for index in (BENEATH_R, ABOVE_R):
                arrived(row_raw.at[index], mat_recv.at[index])
                row_w[index] = stacked(row_raw[index])
            arrived(rhs_row, rhs_recv)
            arrived(row_in.at[0, 1, pl.ds(0, parts - 1)], reduce_recv.at[0, 1])
            arrived(row_in.at[0, 0], reduce_recv.at[0, 0])
            row_x[...] = rhs_row[...] - row_in[0, 1] - row_in[0, 0]

            for j in range(1, ROW_LEVELS):
                @pl.when(level > j)
                def _():
                    arrived(row_in.at[j, 1], reduce_recv.at[j, 1])
                    arrived(row_in.at[j, 0], reduce_recv.at[j, 0])
                    row_x[...] -= row_in[j, 1] + row_in[j, 0]

            row_tall = split_tall(side_by_side(row_x[...]))

            @pl.loop(0, 2)
            def _(turn_id):
                side = jnp.where(odd_pair == 1, turn_id, 1 - turn_id)
                target = e + (2 * side - 1) * reach

                @pl.when(target < slabs)
                def _():
                    row_out[side] = join(times_rows(row_tall, row_w[side]))
                    target_level, _ = place_of(target, levels)
                    send_rows(
                        row_out.at[side],
                        target + 1,
                        target_level > ROW_LEVELS,
                        level,
                        1 - side,
                        up_send.at[side],
                    )

            let_go()

        @pl.when(is_root)
        def _():
            convert(PIVOT)
            product = state_product(PIVOT, state_x[...])
            for k in range(parts):
                solved[k] = product[:, k * rows : (k + 1) * rows]

        @pl.when(not_root)
        def _():
            @pl.when(state_role)
            def _():
                around(
                    s,
                    lambda device: send(
                        state_x, row_x.at[:, states_of(c)], gather_send, gather_recv, device
                    ),
                    skip_own=True,
                )
                row_x[:, states_of(c)] = state_x[...]
                arrived(psi_full.at[pl.ds(0, parts - 1)], gather_recv)

            arrived(row_raw.at[PIVOT], mat_recv.at[PIVOT])
            row_w[PIVOT] = stacked(row_raw[PIVOT])
            pivot_rows[...] = join(
                times_rows(split_tall(side_by_side(row_x[...])), row_w[PIVOT])
            )
            around(
                s,
                lambda device: send(
                    pivot_rows.at[states_of(device[1])], solved.at[c], part_send, part_recv, device
                ),
                skip_own=True,
            )
            solved[c] = pivot_rows[states_of(c)]
            convert_pair(BENEATH_S)
            arrived(rhs_state.at[pl.ds(0, parts - 1)], part_recv)

            @pl.loop(0, 2)
            def _(turn_id):
                side = jnp.where(odd_pair == 1, 1 - turn_id, turn_id)

                @pl.when(e + (2 * side - 1) * reach < slabs)
                def _():
                    arrived(solve_in.at[side], solve_recv.at[side])
                    product = state_product(BENEATH_S + side, solve_in[side])
                    for k in range(parts):
                        solved[k] -= product[:, k * rows : (k + 1) * rows]

        def send_solved(j, side):
            target = s + (2 * side - 1) * jnp.left_shift(jnp.int32(1), j)
            send(
                solved, solve_in.at[1 - side], solve_send.at[j, side],
                solve_recv.at[1 - side], (target, c),
            )

        @pl.loop(0, level - 1)
        def _(i):
            j = level - 1 - i
            send_solved(j, 1)

            @pl.when(not_root)
            def _():
                send_solved(j, 0)

        @pl.when(not_root)
        def _():
            around(
                s - 2,
                lambda device: send(
                    solved, odd_in.at[1, :, states_of(c)], last_send.at[1], last_recv.at[1], device
                ),
            )

        around(
            s,
            lambda device: send(
                solved, odd_in.at[0, :, states_of(c)], last_send.at[0], last_recv.at[0], device
            ),
            skip_own=True,
        )
        odd_in[0, :, states_of(c)] = solved[...]
        around(
            s - 1,
            lambda device: send(
                solved.at[device[1]], out_in.at[states_of(c)], out_send, out_recv, device
            ),
        )

        def settle(side):
            def take():
                if side == 0:
                    arrived(solved_three, last_recv.at[0])
                else:
                    arrived(odd_in.at[1], last_recv.at[1])
                pivot_odd[...] -= join(
                    times_rows(split_tall(side_by_side(odd_in[side])), own_w[BENEATH_S + side])
                )

            if side == 0:
                take()
            else:
                pl.when(has_next)(take)

        solved_three = psi_full.at[pl.ds(0, parts - 1)]

        @pl.when(chip % 2 == 1)
        def _():
            settle(1)
            settle(0)

        @pl.when(chip % 2 == 0)
        def _():
            settle(0)
            settle(1)

        out[0] = pivot_odd[...].T

        arrived(psi_full.at[pl.ds(0, parts - 1)], psi_send)
        arrived(x_full.at[pl.ds(0, parts - 1)], x_send)
        arrived(next_full, next_send)

        @pl.when(state_role)
        def _():
            arrived(rhs_state.at[pl.ds(0, parts - 1)], odd_send.at[0])

        @pl.when(row_role)
        def _():
            arrived(rhs_row.at[pl.ds(0, parts - 1)], odd_send.at[0])

        @pl.when(has_next)
        def _():
            arrived(prev_parts, prev_send)

            @pl.when(level_next > ROW_LEVELS)
            def _():
                arrived(rhs_state, odd_send.at[1])

            @pl.when(level_next <= ROW_LEVELS)
            def _():
                arrived(rhs_row, odd_send.at[1])

        @pl.when(not_root)
        def _():
            @pl.loop(0, 2)
            def _(side):
                target = e + (2 * side - 1) * reach
                target_level, _ = place_of(target, levels)

                @pl.when(target < slabs)
                def _():
                    small = target_level > ROW_LEVELS

                    @pl.when(small)
                    def _():
                        arrived(rhs_state, up_send.at[side])

                    @pl.when(jnp.logical_not(small))
                    def _():
                        arrived(rhs_row, up_send.at[side])

            arrived(rhs_row, last_send.at[1])

        arrived(psi_full.at[pl.ds(0, parts - 1)], last_send.at[0])
        arrived(rhs_state, out_send)

        @pl.when(not_root)
        def _():
            arrived(rhs_state.at[pl.ds(0, parts - 1)], part_send)

            @pl.when(state_role)
            def _():
                arrived(psi_full.at[pl.ds(0, parts - 1)], gather_send)

        @pl.loop(1, level)
        def _(j):
            arrived(solved, solve_send.at[j, 1])

            @pl.when(not_root)
            def _():
                arrived(solved, solve_send.at[j, 0])


def per_device(*args):
    slabs = lax.axis_size("slab")
    levels = slabs.bit_length() - 1
    parts = lax.axis_size("col")
    psi = args[0]
    rows, width = psi.shape[1:]
    depth = parts * rows
    quarter = width // parts
    f32, bf16 = jnp.float32, jnp.bfloat16

    def whole(*lead):
        return pltpu.VMEM((*lead, parts, width, rows), f32)

    def piece(*lead):
        return pltpu.VMEM((*lead, parts, quarter, rows), f32)

    dma = pltpu.SemaphoreType.DMA
    return pl.pallas_call(
        functools.partial(kernel, slabs, levels, parts),
        out_shape=jax.ShapeDtypeStruct(psi.shape, psi.dtype),
        in_specs=[pl.BlockSpec(memory_space=pl.ANY)] * len(args),
        out_specs=pl.BlockSpec(memory_space=pltpu.VMEM),
        scratch_shapes=[
            pltpu.VMEM((rows, width), f32),
            pltpu.VMEM((rows, depth), f32),
            pltpu.VMEM((rows, depth), f32),
            pltpu.VMEM((5, 2, rows, depth), f32),
            pltpu.VMEM((5, 2, depth, rows), f32),
            whole(),
            whole(),
            whole(),
            whole(),
            whole(),
            pltpu.VMEM((2 * rows, depth), bf16),
            pltpu.VMEM((2 * rows, depth), bf16),
            pltpu.VMEM((5, 4 * rows, depth), bf16),
            pltpu.VMEM((3, 2, rows, depth), f32),
            pltpu.VMEM((3, 4 * rows, depth), bf16),
            pltpu.VMEM((5, parts, 2, depth, rows), f32),
            pltpu.VMEM((5, depth, 4 * depth), bf16),
            pltpu.VMEM((width, rows), f32),
            pltpu.VMEM((2, width, rows), f32),
            whole(),
            whole(ROW_LEVELS, 2),
            whole(),
            pltpu.VMEM((2, width, rows), f32),
            piece(),
            piece(levels, 2),
            piece(),
            piece(2),
            piece(2),
            piece(),
            whole(2),
            pltpu.VMEM((width, rows), f32),
            pltpu.VMEM((width, rows), f32),
            dma((8,)),
            *[dma] * 10,
            dma((5,)),
            dma((5,)),
            dma((2,)),
            dma((2,)),
            dma((levels, 2)),
            dma((levels, 2)),
            dma((2,)),
            dma((2,)),
            dma((2,)),
            dma,
            dma,
            *[dma] * 4,
            pltpu.SemaphoreType.REGULAR,
        ],
        compiler_params=pltpu.CompilerParams(
            collective_id=0, has_side_effects=True, vmem_limit_bytes=56 * 2**20
        ),
    )(*args)


def solution(mesh):
    vector = P("slab", "col", None)
    block = P("slab", None, "col", None)
    return jax.shard_map(
        per_device,
        mesh=mesh,
        in_specs=(vector,) * 3 + (block,) * 5,
        out_specs=vector,
        check_vma=False,
    )
```

```python
import functools

import jax
import jax.numpy as jnp
from jax import lax
from jax.experimental import pallas as pl
from jax.experimental.pallas import tpu as pltpu
from jax.sharding import PartitionSpec as P

MESH = pl.DeviceIdType.MESH
half_step = 0.5
ROW_LEVELS = 3
BENEATH_R, ABOVE_R, PIVOT, BENEATH_S, ABOVE_S = range(5)


def rotate(values):
    height = values.shape[0]
    row = lax.broadcasted_iota(jnp.int32, values.shape, 0)
    return jnp.where(
        row % 2 == 0, -pltpu.roll(values, height - 1, 0), pltpu.roll(values, 1, 0)
    )


def split(values):
    high = values.astype(jnp.bfloat16)
    low = (values - high.astype(jnp.float32)).astype(jnp.bfloat16)
    return high, low


def split_tall(values):
    return jnp.concatenate(split(values), axis=0)


def fold(product):
    m, n = product.shape[0] // 2, product.shape[1] // 2
    return product[:m, :n] + (product[m:, :n] + product[:m, n:])


def times_rows(tall, block_rows):
    return fold(
        lax.dot_general(
            tall, block_rows, (((1,), (1,)), ((), ())), preferred_element_type=jnp.float32
        )
    )


def times_columns(tall, block_columns):
    return fold(jnp.dot(tall, block_columns, preferred_element_type=jnp.float32))


def join(both):
    n = both.shape[1] // 2
    return both[:, :n] + rotate(both[:, n:])


def side_by_side(pieces):
    return jnp.concatenate([pieces[k] for k in range(pieces.shape[0])], axis=1)


def place_of(slab, levels):
    level, reach = jnp.int32(0), jnp.int32(1)
    for k in range(1, levels + 1):
        at_least = slab % (2**k) == 0
        level = jnp.where(at_least, k, level)
        reach = jnp.where(at_least, 2**k, reach)
    return level, reach


def kernel(slabs, levels, parts, *refs):
    (
        psi_h, energy_h, tunnel_h, pivot_h, beneath_reduce_h, above_reduce_h,
        beneath_solve_h, above_solve_h, out,
        psi_raw, energy_v, tunnel_v, blocks_v, turned_v,
        psi_full, next_full, prev_parts, prev_send_v, x_full,
        energy_w, tunnel_w, own_w, row_raw, row_w, state_raw, state_w,
        pivot_odd, odd_out,
        rhs_row, row_in, row_x, row_out,
        rhs_state, state_in, state_x, state_out,
        solve_in, solved, odd_in, out_in, pivot_rows,
        load_sem, psi_send, psi_recv, next_send, next_recv, prev_send, prev_recv,
        x_send, x_recv, rhs_send, rhs_recv, mat_send, mat_recv, odd_send, up_send,
        reduce_recv, solve_send, solve_recv, last_send, last_recv, out_send, out_recv,
        gather_send, gather_recv, part_send, part_recv, go,
    ) = refs
    s = lax.axis_index("slab")
    c = lax.axis_index("col")
    odd = s % 2 == 1
    even = s % 2 == 0
    chip = s // 2
    e = chip * 2
    level, reach = place_of(e, levels)
    level_next, _ = place_of(e + 2, levels)
    is_root = e == 0
    not_root = e > 0
    has_above = e + reach < slabs
    state_role = level > ROW_LEVELS
    row_role = level <= ROW_LEVELS
    has_next = e + 2 < slabs
    rows, width = psi_h.shape[1:]
    depth = parts * rows
    quarter = width // parts

    def around(slab, act, skip_own=False):
        for step in (2, 1, 3) if skip_own else (2, 1, 3, 0):
            act((slab, (c + step) % parts))

    def arrived(ref, sem):
        pltpu.make_async_copy(ref, ref, sem).wait()

    def send(source, target, send_sem, recv_sem, device):
        pltpu.make_async_remote_copy(
            src_ref=source, dst_ref=target, send_sem=send_sem, recv_sem=recv_sem,
            device_id=device, device_id_type=MESH,
        ).start()

    def states_of(col):
        return pl.ds(pl.multiple_of(col * quarter, quarter), quarter)

    def load(index, source, target):
        return pltpu.make_async_copy(source, target, load_sem.at[index])

    loads = [
        load(0, psi_h.at[0], psi_raw),
        load(1, tunnel_h.at[0], tunnel_v),
        load(2, energy_h.at[0], energy_v),
        load(3, beneath_reduce_h.at[0], blocks_v.at[BENEATH_R]),
        load(4, above_reduce_h.at[0], blocks_v.at[ABOVE_R]),
        load(5, pivot_h.at[0], blocks_v.at[PIVOT]),
        load(6, beneath_solve_h.at[0], blocks_v.at[BENEATH_S]),
        load(7, above_solve_h.at[0], blocks_v.at[ABOVE_S]),
    ]
    for copy in loads:
        copy.start()

    barrier = pltpu.get_barrier_semaphore()

    def greet(device):
        pl.semaphore_signal(barrier, inc=1, device_id=device, device_id_type=MESH)

    expected = jnp.int32(2 * parts - 1)

    @pl.when(jnp.logical_and(even, not_root))
    def _():
        around(s - 1, greet)

    @pl.when(jnp.logical_and(odd, has_next))
    def _():
        around(s + 1, greet)

    expected += parts * jnp.where(odd, has_next, not_root).astype(jnp.int32)
    around(s + 1 - 2 * (s % 2), greet)
    around(s, greet, skip_own=True)
    for j in range(1, levels):
        for sign in (-1, 1):
            target = s + sign * 2**j
            there = jnp.logical_and(target >= 0, target < slabs)
            if j > 1:
                there = jnp.logical_and(there, j <= level)
            there = jnp.logical_and(there, odd)
            count = parts if j <= max(ROW_LEVELS, 1) else 1
            expected += count * there.astype(jnp.int32)

            @pl.when(there)
            def _():
                if count > 1:
                    around(target, greet)
                else:
                    greet((target, c))

    loads[0].wait()
    loads[1].wait()
    own = psi_raw[...].T
    psi_full[c] = own
    tunnel = tunnel_v[...]
    wide_tunnel = jnp.concatenate(split(tunnel), axis=1)
    partial = times_columns(split_tall(own), wide_tunnel)
    for k in range(parts):
        prev_send_v[k] = partial[:, k * rows : (k + 1) * rows]

    pl.semaphore_wait(barrier, expected)

    def send_psi_row():
        around(
            s,
            lambda device: send(psi_full.at[c], psi_full.at[c], psi_send, psi_recv, device),
            skip_own=True,
        )

    def send_prev():
        around(
            s + 1,
            lambda device: send(
                prev_send_v.at[device[1]], prev_parts.at[c], prev_send, prev_recv, device
            ),
        )

    @pl.when(odd)
    def _():
        send_psi_row()

    @pl.when(even)
    def _():
        @pl.when(not_root)
        def _():
            around(
                s - 1,
                lambda device: send(
                    psi_full.at[c], next_full.at[c], next_send, next_recv, device
                ),
            )

        send_prev()
        send_psi_row()

    def stacked(block):
        return split_tall(block.reshape(2 * rows, depth))

    tunnel_w[...] = split_tall(tunnel)
    loads[2].wait()
    energy_w[...] = split_tall(energy_v[...])
    for index in range(5):
        loads[3 + index].wait()

    def turn(index):
        for part in range(2):
            turned_v[index, part] = blocks_v[index, part].T

    def pass_on(index):
        around(
            s + 1,
            lambda device: send(
                turned_v.at[index],
                state_raw.at[index, c],
                mat_send.at[index],
                mat_recv.at[index],
                device,
            ),
        )

    def hand_over(index):
        send(
            blocks_v.at[index], row_raw.at[index], mat_send.at[index], mat_recv.at[index],
            (s + 1, c),
        )

    @pl.when(even)
    def _():
        @pl.when(is_root)
        def _():
            turn(PIVOT)
            pass_on(PIVOT)

        @pl.when(not_root)
        def _():
            hand_over(PIVOT)

            @pl.when(row_role)
            def _():
                hand_over(BENEATH_R)
                hand_over(ABOVE_R)

            @pl.when(state_role)
            def _():
                turn(BENEATH_R)
                pass_on(BENEATH_R)

                @pl.when(has_above)
                def _():
                    turn(ABOVE_R)
                    pass_on(ABOVE_R)

    @pl.when(odd)
    def _():
        own_w[BENEATH_R] = stacked(blocks_v[BENEATH_R])
        own_w[ABOVE_R] = stacked(blocks_v[ABOVE_R])

    arrived(psi_full.at[pl.ds(0, parts - 1)], psi_recv)
    x_full[c] = times_rows(split_tall(side_by_side(psi_full[...])), energy_w[...])

    @pl.when(s > 0)
    def _():
        arrived(prev_parts, prev_recv)
        x_full[c] += (prev_parts[0] + prev_parts[1]) + (prev_parts[2] + prev_parts[3])

    @pl.when(s + 1 < slabs)
    def _():
        arrived(next_full, next_recv)
        x_full[c] += times_rows(split_tall(side_by_side(next_full[...])), tunnel_w[...])

    x_full[c] = psi_full[c] - half_step * rotate(x_full[c])

    @pl.when(even)
    def _():
        @pl.when(state_role)
        def _():
            around(
                s + 1,
                lambda device: send(
                    x_full.at[c, states_of(device[1])], rhs_state.at[c], rhs_send, rhs_recv, device
                ),
            )

        @pl.when(row_role)
        def _():
            around(
                s + 1,
                lambda device: send(x_full.at[c], rhs_row.at[c], rhs_send, rhs_recv, device),
            )

        @pl.when(not_root)
        def _():
            turn(BENEATH_S)
            turn(ABOVE_S)

        pl.semaphore_wait(go, 1)

        @pl.when(not_root)
        def _():
            pass_on(BENEATH_S)

            @pl.when(has_above)
            def _():
                pass_on(ABOVE_S)

        arrived(out_in, out_recv)
        out[0] = out_in[...].T

        arrived(psi_full.at[pl.ds(0, parts - 1)], psi_send)
        arrived(prev_parts, prev_send)

        @pl.when(not_root)
        def _():
            arrived(next_full, next_send)
            arrived(state_raw.at[BENEATH_S], mat_send.at[BENEATH_S])
            arrived(row_raw.at[PIVOT], mat_send.at[PIVOT])

            @pl.when(has_above)
            def _():
                arrived(state_raw.at[ABOVE_S], mat_send.at[ABOVE_S])

            @pl.when(state_role)
            def _():
                arrived(state_raw.at[BENEATH_R], mat_send.at[BENEATH_R])

                @pl.when(has_above)
                def _():
                    arrived(state_raw.at[ABOVE_R], mat_send.at[ABOVE_R])

            @pl.when(row_role)
            def _():
                arrived(row_raw.at[BENEATH_R], mat_send.at[BENEATH_R])
                arrived(row_raw.at[ABOVE_R], mat_send.at[ABOVE_R])

        @pl.when(is_root)
        def _():
            arrived(state_raw.at[PIVOT], mat_send.at[PIVOT])

        @pl.when(state_role)
        def _():
            arrived(rhs_state, rhs_send)

        @pl.when(row_role)
        def _():
            arrived(rhs_row, rhs_send)

    @pl.when(odd)
    def _():
        around(
            s,
            lambda device: send(x_full.at[c], x_full.at[c], x_send, x_recv, device),
            skip_own=True,
        )
        send(psi_full, next_full, next_send, next_recv, (s - 1, c))

        @pl.when(has_next)
        def _():
            send_prev()

        own_w[PIVOT] = stacked(blocks_v[PIVOT])
        own_w[BENEATH_S] = stacked(blocks_v[BENEATH_S])
        own_w[ABOVE_S] = stacked(blocks_v[ABOVE_S])

        arrived(x_full.at[pl.ds(0, parts - 1)], x_recv)
        tall = split_tall(side_by_side(x_full[...]))

        def send_rows(source, host, to_state, tier, side, sem, skip_own=False):
            @pl.when(to_state)
            def _():
                around(
                    host,
                    lambda device: send(
                        source.at[states_of(device[1])],
                        state_in.at[tier, side, c],
                        sem,
                        reduce_recv.at[tier, side],
                        device,
                    ),
                    skip_own,
                )

            @pl.when(jnp.logical_not(to_state))
            def _():
                around(
                    host,
                    lambda device: send(
                        source,
                        row_in.at[jnp.minimum(tier, ROW_LEVELS - 1), side, c],
                        sem,
                        reduce_recv.at[tier, side],
                        device,
                    ),
                    skip_own,
                )

        def odd_beneath():
            odd_out[0] = join(times_rows(tall, own_w[BENEATH_R]))
            send_rows(odd_out.at[0], s, state_role, 0, 1, odd_send.at[0], skip_own=True)

            @pl.when(state_role)
            def _():
                state_in[0, 1, c] = odd_out[0, states_of(c)]

            @pl.when(row_role)
            def _():
                row_in[0, 1, c] = odd_out[0]

        def odd_above():
            @pl.when(has_next)
            def _():
                odd_out[1] = join(times_rows(tall, own_w[ABOVE_R]))
                send_rows(
                    odd_out.at[1], s + 2, level_next > ROW_LEVELS, 0, 0, odd_send.at[1]
                )

        @pl.when(chip % 2 == 1)
        def _():
            odd_beneath()
            odd_above()

        @pl.when(chip % 2 == 0)
        def _():
            odd_above()
            odd_beneath()

        def let_go():
            pl.semaphore_signal(go, inc=1, device_id=(s - 1, c), device_id_type=MESH)

        @pl.when(state_role)
        def _():
            let_go()

        pivot_odd[...] = join(times_rows(tall, own_w[PIVOT]))

        odd_pair = (e // reach // 2) % 2

        pieces = parts // 2

        def convert(index):
            arrived(state_raw.at[index], mat_recv.at[index])
            for part in range(2):
                for k in range(parts):
                    half, place = k // pieces, k % pieces
                    at = (part * pieces + place) * rows
                    high, low = split(state_raw[index, k, part])
                    state_w[index, half, :, at : at + rows] = high
                    state_w[index, half, :, depth + at : depth + at + rows] = low

        def convert_pair(first):
            @pl.loop(first, first + 1 + has_above.astype(jnp.int32))
            def _(index):
                convert(index)

        def by_halves(index, vectors, take):
            tall = split_tall(side_by_side(vectors))
            for half in range(2):
                product = join(times_columns(tall, state_w[index, half]))
                for place in range(pieces):
                    take(half * pieces + place, product[:, place * rows : (place + 1) * rows])
                yield pl.ds(half * pieces, pieces)

        @pl.when(state_role)
        def _():
            @pl.when(not_root)
            def _():
                convert_pair(BENEATH_R)

            arrived(rhs_state, rhs_recv)
            arrived(state_in.at[0, 1, pl.ds(0, parts - 1)], reduce_recv.at[0, 1])
            state_x[...] = rhs_state[...] - state_in[0, 1]

            @pl.when(not_root)
            def _():
                arrived(state_in.at[0, 0], reduce_recv.at[0, 0])
                state_x[...] -= state_in[0, 0]

            @pl.loop(1, level)
            def _(j):
                arrived(state_in.at[j, 1], reduce_recv.at[j, 1])
                state_x[...] -= state_in[j, 1]

                @pl.when(not_root)
                def _():
                    arrived(state_in.at[j, 0], reduce_recv.at[j, 0])
                    state_x[...] -= state_in[j, 0]

            @pl.when(not_root)
            def _():
                @pl.loop(0, 2)
                def _(turn_id):
                    side = jnp.where(odd_pair == 1, turn_id, 1 - turn_id)
                    target = e + (2 * side - 1) * reach

                    @pl.when(target < slabs)
                    def _():
                        def put(k, product):
                            state_out[side, k] = product

                        for half in by_halves(side, state_x[...], put):
                            send(
                                state_out.at[side, half],
                                state_in.at[level, 1 - side, half],
                                up_send.at[side],
                                reduce_recv.at[level, 1 - side],
                                (target + 1, c),
                            )

        @pl.when(row_role)
        def _():
            for index in (BENEATH_R, ABOVE_R):
                arrived(row_raw.at[index], mat_recv.at[index])
                row_w[index] = stacked(row_raw[index])
            arrived(rhs_row, rhs_recv)
            arrived(row_in.at[0, 1, pl.ds(0, parts - 1)], reduce_recv.at[0, 1])
            arrived(row_in.at[0, 0], reduce_recv.at[0, 0])
            row_x[...] = rhs_row[...] - row_in[0, 1] - row_in[0, 0]

            for j in range(1, ROW_LEVELS):
                @pl.when(level > j)
                def _():
                    arrived(row_in.at[j, 1], reduce_recv.at[j, 1])
                    arrived(row_in.at[j, 0], reduce_recv.at[j, 0])
                    row_x[...] -= row_in[j, 1] + row_in[j, 0]

            row_tall = split_tall(side_by_side(row_x[...]))

            @pl.loop(0, 2)
            def _(turn_id):
                side = jnp.where(odd_pair == 1, turn_id, 1 - turn_id)
                target = e + (2 * side - 1) * reach

                @pl.when(target < slabs)
                def _():
                    row_out[side] = join(times_rows(row_tall, row_w[side]))
                    target_level, _ = place_of(target, levels)
                    send_rows(
                        row_out.at[side],
                        target + 1,
                        target_level > ROW_LEVELS,
                        level,
                        1 - side,
                        up_send.at[side],
                    )

            let_go()

        def send_solved(j, side, half):
            target = s + (2 * side - 1) * jnp.left_shift(jnp.int32(1), j)
            send(
                solved.at[half], solve_in.at[1 - side, half], solve_send.at[j, side],
                solve_recv.at[1 - side], (target, c),
            )

        def send_tier(j, half):
            send_solved(j, 1, half)

            @pl.when(not_root)
            def _():
                send_solved(j, 0, half)

        def first_tier(half):
            @pl.when(level > 1)
            def _():
                send_tier(level - 1, half)

        def put_solved(k, product):
            solved[k] = product

        def take_off(k, product):
            solved[k] -= product

        @pl.when(is_root)
        def _():
            convert(PIVOT)
            for half in by_halves(PIVOT, state_x[...], put_solved):
                first_tier(half)

        @pl.when(not_root)
        def _():
            @pl.when(state_role)
            def _():
                around(
                    s,
                    lambda device: send(
                        state_x, row_x.at[:, states_of(c)], gather_send, gather_recv, device
                    ),
                    skip_own=True,
                )
                row_x[:, states_of(c)] = state_x[...]
                arrived(psi_full.at[pl.ds(0, parts - 1)], gather_recv)

            arrived(row_raw.at[PIVOT], mat_recv.at[PIVOT])
            row_w[PIVOT] = stacked(row_raw[PIVOT])
            pivot_rows[...] = join(
                times_rows(split_tall(side_by_side(row_x[...])), row_w[PIVOT])
            )
            around(
                s,
                lambda device: send(
                    pivot_rows.at[states_of(device[1])], solved.at[c], part_send, part_recv, device
                ),
                skip_own=True,
            )
            solved[c] = pivot_rows[states_of(c)]
            convert_pair(BENEATH_S)
            arrived(rhs_state.at[pl.ds(0, parts - 1)], part_recv)

            early = jnp.where(jnp.logical_or(odd_pair == 1, jnp.logical_not(has_above)), 1, 0)
            last = 1 - early

            @pl.when(jnp.logical_or(early == 0, has_above))
            def _():
                arrived(solve_in.at[early], solve_recv.at[early])
                for _ in by_halves(BENEATH_S + early, solve_in[early], take_off):
                    pass

            arrived(solve_in.at[last], solve_recv.at[last])
            for half in by_halves(BENEATH_S + last, solve_in[last], take_off):
                first_tier(half)

        @pl.loop(1, level - 1)
        def _(i):
            send_tier(level - 1 - i, pl.ds(0, parts))

        @pl.when(not_root)
        def _():
            around(
                s - 2,
                lambda device: send(
                    solved, odd_in.at[1, :, states_of(c)], last_send.at[1], last_recv.at[1], device
                ),
            )

        around(
            s,
            lambda device: send(
                solved, odd_in.at[0, :, states_of(c)], last_send.at[0], last_recv.at[0], device
            ),
            skip_own=True,
        )
        odd_in[0, :, states_of(c)] = solved[...]
        around(
            s - 1,
            lambda device: send(
                solved.at[device[1]], out_in.at[states_of(c)], out_send, out_recv, device
            ),
        )

        def settle(side):
            def take():
                if side == 0:
                    arrived(solved_three, last_recv.at[0])
                else:
                    arrived(odd_in.at[1], last_recv.at[1])
                pivot_odd[...] -= join(
                    times_rows(split_tall(side_by_side(odd_in[side])), own_w[BENEATH_S + side])
                )

            if side == 0:
                take()
            else:
                pl.when(has_next)(take)

        solved_three = psi_full.at[pl.ds(0, parts - 1)]

        @pl.when(chip % 2 == 1)
        def _():
            settle(1)
            settle(0)

        @pl.when(chip % 2 == 0)
        def _():
            settle(0)
            settle(1)

        out[0] = pivot_odd[...].T

        arrived(psi_full.at[pl.ds(0, parts - 1)], psi_send)
        arrived(x_full.at[pl.ds(0, parts - 1)], x_send)
        arrived(next_full, next_send)

        @pl.when(state_role)
        def _():
            arrived(rhs_state.at[pl.ds(0, parts - 1)], odd_send.at[0])

        @pl.when(row_role)
        def _():
            arrived(rhs_row.at[pl.ds(0, parts - 1)], odd_send.at[0])

        @pl.when(has_next)
        def _():
            arrived(prev_parts, prev_send)

            @pl.when(level_next > ROW_LEVELS)
            def _():
                arrived(rhs_state, odd_send.at[1])

            @pl.when(level_next <= ROW_LEVELS)
            def _():
                arrived(rhs_row, odd_send.at[1])

        @pl.when(not_root)
        def _():
            @pl.loop(0, 2)
            def _(side):
                target = e + (2 * side - 1) * reach
                target_level, _ = place_of(target, levels)

                @pl.when(target < slabs)
                def _():
                    small = target_level > ROW_LEVELS

                    @pl.when(small)
                    def _():
                        arrived(rhs_state, up_send.at[side])

                    @pl.when(jnp.logical_not(small))
                    def _():
                        arrived(rhs_row, up_send.at[side])

            arrived(rhs_row, last_send.at[1])

        arrived(psi_full.at[pl.ds(0, parts - 1)], last_send.at[0])
        arrived(rhs_state, out_send)

        @pl.when(not_root)
        def _():
            arrived(rhs_state.at[pl.ds(0, parts - 1)], part_send)

            @pl.when(state_role)
            def _():
                arrived(psi_full.at[pl.ds(0, parts - 1)], gather_send)

        @pl.loop(1, level)
        def _(j):
            arrived(solved, solve_send.at[j, 1])

            @pl.when(not_root)
            def _():
                arrived(solved, solve_send.at[j, 0])


def per_device(*args):
    slabs = lax.axis_size("slab")
    levels = slabs.bit_length() - 1
    parts = lax.axis_size("col")
    psi = args[0]
    rows, width = psi.shape[1:]
    depth = parts * rows
    quarter = width // parts
    f32, bf16 = jnp.float32, jnp.bfloat16

    def whole(*lead):
        return pltpu.VMEM((*lead, parts, width, rows), f32)

    def piece(*lead):
        return pltpu.VMEM((*lead, parts, quarter, rows), f32)

    dma = pltpu.SemaphoreType.DMA
    return pl.pallas_call(
        functools.partial(kernel, slabs, levels, parts),
        out_shape=jax.ShapeDtypeStruct(psi.shape, psi.dtype),
        in_specs=[pl.BlockSpec(memory_space=pl.ANY)] * len(args),
        out_specs=pl.BlockSpec(memory_space=pltpu.VMEM),
        scratch_shapes=[
            pltpu.VMEM((rows, width), f32),
            pltpu.VMEM((rows, depth), f32),
            pltpu.VMEM((rows, depth), f32),
            pltpu.VMEM((5, 2, rows, depth), f32),
            pltpu.VMEM((5, 2, depth, rows), f32),
            whole(),
            whole(),
            whole(),
            whole(),
            whole(),
            pltpu.VMEM((2 * rows, depth), bf16),
            pltpu.VMEM((2 * rows, depth), bf16),
            pltpu.VMEM((5, 4 * rows, depth), bf16),
            pltpu.VMEM((3, 2, rows, depth), f32),
            pltpu.VMEM((3, 4 * rows, depth), bf16),
            pltpu.VMEM((5, parts, 2, depth, rows), f32),
            pltpu.VMEM((5, 2, depth, 2 * depth), bf16),
            pltpu.VMEM((width, rows), f32),
            pltpu.VMEM((2, width, rows), f32),
            whole(),
            whole(ROW_LEVELS, 2),
            whole(),
            pltpu.VMEM((2, width, rows), f32),
            piece(),
            piece(levels, 2),
            piece(),
            piece(2),
            piece(2),
            piece(),
            whole(2),
            pltpu.VMEM((width, rows), f32),
            pltpu.VMEM((width, rows), f32),
            dma((8,)),
            *[dma] * 10,
            dma((5,)),
            dma((5,)),
            dma((2,)),
            dma((2,)),
            dma((levels, 2)),
            dma((levels, 2)),
            dma((2,)),
            dma((2,)),
            dma((2,)),
            dma,
            dma,
            *[dma] * 4,
            pltpu.SemaphoreType.REGULAR,
        ],
        compiler_params=pltpu.CompilerParams(
            collective_id=0, has_side_effects=True, vmem_limit_bytes=56 * 2**20
        ),
    )(*args)


def solution(mesh):
    vector = P("slab", "col", None)
    block = P("slab", None, "col", None)
    return jax.shard_map(
        per_device,
        mesh=mesh,
        in_specs=(vector,) * 3 + (block,) * 5,
        out_specs=vector,
        check_vma=False,
    )
```

```python
import functools

import jax
import jax.numpy as jnp
from jax import lax
from jax.experimental import pallas as pl
from jax.experimental.pallas import tpu as pltpu
from jax.sharding import PartitionSpec as P

MESH = pl.DeviceIdType.MESH
half_step = 0.5
ROW_LEVELS = 2
BENEATH_R, ABOVE_R, PIVOT, BENEATH_S, ABOVE_S = range(5)


def rotate(values):
    height = values.shape[0]
    row = lax.broadcasted_iota(jnp.int32, values.shape, 0)
    return jnp.where(
        row % 2 == 0, -pltpu.roll(values, height - 1, 0), pltpu.roll(values, 1, 0)
    )


def split(values):
    high = values.astype(jnp.bfloat16)
    low = (values - high.astype(jnp.float32)).astype(jnp.bfloat16)
    return high, low


def split_tall(values):
    return jnp.concatenate(split(values), axis=0)


def fold(product):
    m, n = product.shape[0] // 2, product.shape[1] // 2
    return product[:m, :n] + (product[m:, :n] + product[:m, n:])


def times_rows(tall, block_rows):
    return fold(
        lax.dot_general(
            tall, block_rows, (((1,), (1,)), ((), ())), preferred_element_type=jnp.float32
        )
    )


def times_columns(tall, block_columns):
    return fold(jnp.dot(tall, block_columns, preferred_element_type=jnp.float32))


def join(both):
    n = both.shape[1] // 2
    return both[:, :n] + rotate(both[:, n:])


def side_by_side(pieces):
    return jnp.concatenate([pieces[k] for k in range(pieces.shape[0])], axis=1)


def place_of(slab, levels):
    level, reach = jnp.int32(0), jnp.int32(1)
    for k in range(1, levels + 1):
        at_least = slab % (2**k) == 0
        level = jnp.where(at_least, k, level)
        reach = jnp.where(at_least, 2**k, reach)
    return level, reach


def kernel(slabs, levels, parts, *refs):
    (
        psi_h, energy_h, tunnel_h, pivot_h, beneath_reduce_h, above_reduce_h,
        beneath_solve_h, above_solve_h, out,
        psi_raw, energy_v, tunnel_v, blocks_v, turned_v,
        psi_full, tunnel_in, up_rows, up_in, prev_parts, prev_send_v, x_full,
        energy_w, tunnel_w, own_w, row_raw, row_w, state_raw, state_w,
        pivot_odd, odd_out,
        rhs_row, row_in, row_x, row_out,
        rhs_state, state_in, state_x, state_out,
        solve_in, solved, odd_in, out_in, pivot_rows,
        load_sem, psi_send, psi_recv, next_send, next_recv, prev_send, prev_recv,
        x_send, x_recv, rhs_send, rhs_recv, mat_send, mat_recv, odd_send, up_send,
        reduce_recv, solve_send, solve_recv, last_send, last_recv, out_send, out_recv,
        gather_send, gather_recv, part_send, part_recv, serve_send, serve_recv, go,
    ) = refs
    s = lax.axis_index("slab")
    c = lax.axis_index("col")
    odd = s % 2 == 1
    even = s % 2 == 0
    chip = s // 2
    e = chip * 2
    level, reach = place_of(e, levels)
    level_next, _ = place_of(e + 2, levels)
    is_root = e == 0
    not_root = e > 0
    has_above = e + reach < slabs
    state_role = level > ROW_LEVELS
    row_role = level <= ROW_LEVELS
    has_next = e + 2 < slabs
    rows, width = psi_h.shape[1:]
    depth = parts * rows
    quarter = width // parts

    def around(slab, act, skip_own=False):
        for step in (2, 1, 3) if skip_own else (2, 1, 3, 0):
            act((slab, (c + step) % parts))

    def arrived(ref, sem):
        pltpu.make_async_copy(ref, ref, sem).wait()

    def send(source, target, send_sem, recv_sem, device):
        pltpu.make_async_remote_copy(
            src_ref=source, dst_ref=target, send_sem=send_sem, recv_sem=recv_sem,
            device_id=device, device_id_type=MESH,
        ).start()

    def states_of(col):
        return pl.ds(pl.multiple_of(col * quarter, quarter), quarter)

    def load(index, source, target):
        return pltpu.make_async_copy(source, target, load_sem.at[index])

    loads = [
        load(0, psi_h.at[0], psi_raw),
        load(1, tunnel_h.at[0], tunnel_v),
        load(2, energy_h.at[0], energy_v),
        load(3, beneath_reduce_h.at[0], blocks_v.at[BENEATH_R]),
        load(4, above_reduce_h.at[0], blocks_v.at[ABOVE_R]),
        load(5, pivot_h.at[0], blocks_v.at[PIVOT]),
        load(6, beneath_solve_h.at[0], blocks_v.at[BENEATH_S]),
        load(7, above_solve_h.at[0], blocks_v.at[ABOVE_S]),
    ]
    for copy in loads:
        copy.start()

    barrier = pltpu.get_barrier_semaphore()

    def greet(device):
        pl.semaphore_signal(barrier, inc=1, device_id=device, device_id_type=MESH)

    expected = jnp.int32(2 * parts - 1)

    @pl.when(jnp.logical_and(even, not_root))
    def _():
        around(s - 1, greet)

    @pl.when(jnp.logical_and(odd, has_next))
    def _():
        around(s + 1, greet)

    expected += parts * jnp.where(odd, has_next, not_root).astype(jnp.int32)
    around(s + 1 - 2 * (s % 2), greet)
    around(s, greet, skip_own=True)
    for j in range(1, levels):
        for sign in (-1, 1):
            target = s + sign * 2**j
            there = jnp.logical_and(target >= 0, target < slabs)
            if j > 1:
                there = jnp.logical_and(there, j <= level)
            there = jnp.logical_and(there, odd)
            count = parts if j <= max(ROW_LEVELS, 1) else 1
            expected += count * there.astype(jnp.int32)

            @pl.when(there)
            def _():
                if count > 1:
                    around(target, greet)
                else:
                    greet((target, c))

    loads[0].wait()
    loads[1].wait()
    own = psi_raw[...].T
    psi_full[c] = own
    tunnel = tunnel_v[...]
    wide_tunnel = jnp.concatenate(split(tunnel), axis=1)
    partial = times_columns(split_tall(own), wide_tunnel)
    for k in range(parts):
        prev_send_v[k] = partial[:, k * rows : (k + 1) * rows]

    pl.semaphore_wait(barrier, expected)

    def send_psi_row():
        around(
            s,
            lambda device: send(psi_full.at[c], psi_full.at[c], psi_send, psi_recv, device),
            skip_own=True,
        )

    def send_prev():
        around(
            s + 1,
            lambda device: send(
                prev_send_v.at[device[1]], prev_parts.at[c], prev_send, prev_recv, device
            ),
        )

    def send_tunnel():
        send(tunnel_v, tunnel_in, next_send, next_recv, (s + 1, c))

    @pl.when(odd)
    def _():
        @pl.when(has_next)
        def _():
            send_tunnel()

        send_psi_row()

    @pl.when(even)
    def _():
        send_psi_row()
        send_prev()
        send_tunnel()

    def stacked(block):
        return split_tall(block.reshape(2 * rows, depth))

    loads[2].wait()
    energy_w[...] = split_tall(energy_v[...])
    for index in range(5):
        loads[3 + index].wait()

    def turn(index):
        for part in range(2):
            turned_v[index, part] = blocks_v[index, part].T

    def pass_on(index):
        around(
            s + 1,
            lambda device: send(
                turned_v.at[index],
                state_raw.at[index, c],
                mat_send.at[index],
                mat_recv.at[index],
                device,
            ),
        )

    def hand_over(index):
        send(
            blocks_v.at[index], row_raw.at[index], mat_send.at[index], mat_recv.at[index],
            (s + 1, c),
        )

    @pl.when(even)
    def _():
        @pl.when(is_root)
        def _():
            turn(PIVOT)
            pass_on(PIVOT)

        @pl.when(not_root)
        def _():
            hand_over(PIVOT)

            @pl.when(row_role)
            def _():
                hand_over(BENEATH_R)
                hand_over(ABOVE_R)

            @pl.when(state_role)
            def _():
                turn(BENEATH_R)
                pass_on(BENEATH_R)

                @pl.when(has_above)
                def _():
                    turn(ABOVE_R)
                    pass_on(ABOVE_R)

    @pl.when(odd)
    def _():
        own_w[BENEATH_R] = stacked(blocks_v[BENEATH_R])
        own_w[ABOVE_R] = stacked(blocks_v[ABOVE_R])

    arrived(psi_full.at[pl.ds(0, parts - 1)], psi_recv)
    psi_tall = split_tall(side_by_side(psi_full[...]))

    def serve_beneath():
        arrived(tunnel_in, next_recv)
        tunnel_w[...] = split_tall(tunnel_in[...])
        up_rows[...] = times_rows(psi_tall, tunnel_w[...])
        send(up_rows, up_in, serve_send, serve_recv, (s - 1, c))

    @pl.when(jnp.logical_and(even, not_root))
    def _():
        serve_beneath()

    x_full[c] = times_rows(psi_tall, energy_w[...])

    @pl.when(s > 0)
    def _():
        arrived(prev_parts, prev_recv)
        x_full[c] += (prev_parts[0] + prev_parts[1]) + (prev_parts[2] + prev_parts[3])

    @pl.when(s + 1 < slabs)
    def _():
        arrived(up_in, serve_recv)
        x_full[c] += up_in[...]

    x_full[c] = psi_full[c] - half_step * rotate(x_full[c])

    @pl.when(even)
    def _():
        @pl.when(state_role)
        def _():
            around(
                s + 1,
                lambda device: send(
                    x_full.at[c, states_of(device[1])], rhs_state.at[c], rhs_send, rhs_recv, device
                ),
            )

        @pl.when(row_role)
        def _():
            around(
                s + 1,
                lambda device: send(x_full.at[c], rhs_row.at[c], rhs_send, rhs_recv, device),
            )

        @pl.when(not_root)
        def _():
            turn(BENEATH_S)
            turn(ABOVE_S)

        pl.semaphore_wait(go, 1)

        @pl.when(not_root)
        def _():
            pass_on(BENEATH_S)

            @pl.when(has_above)
            def _():
                pass_on(ABOVE_S)

        arrived(out_in, out_recv)
        out[0] = out_in[...].T

        arrived(psi_full.at[pl.ds(0, parts - 1)], psi_send)
        arrived(prev_parts, prev_send)
        arrived(tunnel_in, next_send)

        @pl.when(not_root)
        def _():
            arrived(up_in, serve_send)
            arrived(state_raw.at[BENEATH_S], mat_send.at[BENEATH_S])
            arrived(row_raw.at[PIVOT], mat_send.at[PIVOT])

            @pl.when(has_above)
            def _():
                arrived(state_raw.at[ABOVE_S], mat_send.at[ABOVE_S])

            @pl.when(state_role)
            def _():
                arrived(state_raw.at[BENEATH_R], mat_send.at[BENEATH_R])

                @pl.when(has_above)
                def _():
                    arrived(state_raw.at[ABOVE_R], mat_send.at[ABOVE_R])

            @pl.when(row_role)
            def _():
                arrived(row_raw.at[BENEATH_R], mat_send.at[BENEATH_R])
                arrived(row_raw.at[ABOVE_R], mat_send.at[ABOVE_R])

        @pl.when(is_root)
        def _():
            arrived(state_raw.at[PIVOT], mat_send.at[PIVOT])

        @pl.when(state_role)
        def _():
            arrived(rhs_state, rhs_send)

        @pl.when(row_role)
        def _():
            arrived(rhs_row, rhs_send)

    @pl.when(odd)
    def _():
        around(
            s,
            lambda device: send(x_full.at[c], x_full.at[c], x_send, x_recv, device),
            skip_own=True,
        )
        serve_beneath()

        @pl.when(has_next)
        def _():
            send_prev()

        own_w[PIVOT] = stacked(blocks_v[PIVOT])
        own_w[BENEATH_S] = stacked(blocks_v[BENEATH_S])
        own_w[ABOVE_S] = stacked(blocks_v[ABOVE_S])

        arrived(x_full.at[pl.ds(0, parts - 1)], x_recv)
        tall = split_tall(side_by_side(x_full[...]))

        def send_rows(source, host, to_state, tier, side, sem, skip_own=False):
            @pl.when(to_state)
            def _():
                around(
                    host,
                    lambda device: send(
                        source.at[states_of(device[1])],
                        state_in.at[tier, side, c],
                        sem,
                        reduce_recv.at[tier, side],
                        device,
                    ),
                    skip_own,
                )

            @pl.when(jnp.logical_not(to_state))
            def _():
                around(
                    host,
                    lambda device: send(
                        source,
                        row_in.at[jnp.minimum(tier, ROW_LEVELS - 1), side, c],
                        sem,
                        reduce_recv.at[tier, side],
                        device,
                    ),
                    skip_own,
                )

        def odd_beneath():
            odd_out[0] = join(times_rows(tall, own_w[BENEATH_R]))
            send_rows(odd_out.at[0], s, state_role, 0, 1, odd_send.at[0], skip_own=True)

            @pl.when(state_role)
            def _():
                state_in[0, 1, c] = odd_out[0, states_of(c)]

            @pl.when(row_role)
            def _():
                row_in[0, 1, c] = odd_out[0]

        def odd_above():
            @pl.when(has_next)
            def _():
                odd_out[1] = join(times_rows(tall, own_w[ABOVE_R]))
                send_rows(
                    odd_out.at[1], s + 2, level_next > ROW_LEVELS, 0, 0, odd_send.at[1]
                )

        def sent_beneath():
            @pl.when(state_role)
            def _():
                arrived(rhs_state.at[pl.ds(0, parts - 1)], odd_send.at[0])

            @pl.when(row_role)
            def _():
                arrived(rhs_row.at[pl.ds(0, parts - 1)], odd_send.at[0])

        def sent_above():
            @pl.when(jnp.logical_and(has_next, level_next > ROW_LEVELS))
            def _():
                arrived(rhs_state, odd_send.at[1])

            @pl.when(jnp.logical_and(has_next, level_next <= ROW_LEVELS))
            def _():
                arrived(rhs_row, odd_send.at[1])

        @pl.when(chip % 2 == 1)
        def _():
            odd_beneath()
            sent_beneath()
            odd_above()

        @pl.when(chip % 2 == 0)
        def _():
            odd_above()
            sent_above()
            odd_beneath()

        def sent_up(side):
            target = e + (2 * side - 1) * reach
            target_level, _ = place_of(target, levels)
            small = target_level > ROW_LEVELS

            @pl.when(jnp.logical_and(target < slabs, small))
            def _():
                arrived(rhs_state, up_send.at[side])

            @pl.when(jnp.logical_and(target < slabs, jnp.logical_not(small)))
            def _():
                arrived(rhs_row, up_send.at[side])

        def let_go():
            pl.semaphore_signal(go, inc=1, device_id=(s - 1, c), device_id_type=MESH)

        @pl.when(state_role)
        def _():
            let_go()

        pivot_odd[...] = join(times_rows(tall, own_w[PIVOT]))

        odd_pair = (e // reach // 2) % 2

        pieces = parts // 2

        def convert(index):
            arrived(state_raw.at[index], mat_recv.at[index])
            for part in range(2):
                for k in range(parts):
                    half, place = k // pieces, k % pieces
                    at = (part * pieces + place) * rows
                    high, low = split(state_raw[index, k, part])
                    state_w[index, half, :, at : at + rows] = high
                    state_w[index, half, :, depth + at : depth + at + rows] = low

        def convert_pair(first):
            @pl.loop(first, first + 1 + has_above.astype(jnp.int32))
            def _(index):
                convert(index)

        def by_halves(index, vectors, take):
            tall = split_tall(side_by_side(vectors))
            for half in range(2):
                product = join(times_columns(tall, state_w[index, half]))
                for place in range(pieces):
                    take(half * pieces + place, product[:, place * rows : (place + 1) * rows])
                yield pl.ds(half * pieces, pieces)

        @pl.when(state_role)
        def _():
            @pl.when(not_root)
            def _():
                convert_pair(BENEATH_R)

            arrived(rhs_state, rhs_recv)
            arrived(state_in.at[0, 1, pl.ds(0, parts - 1)], reduce_recv.at[0, 1])
            state_x[...] = rhs_state[...] - state_in[0, 1]

            @pl.when(not_root)
            def _():
                arrived(state_in.at[0, 0], reduce_recv.at[0, 0])
                state_x[...] -= state_in[0, 0]

            @pl.loop(1, level)
            def _(j):
                arrived(state_in.at[j, 1], reduce_recv.at[j, 1])
                state_x[...] -= state_in[j, 1]

                @pl.when(not_root)
                def _():
                    arrived(state_in.at[j, 0], reduce_recv.at[j, 0])
                    state_x[...] -= state_in[j, 0]

            @pl.when(not_root)
            def _():
                @pl.loop(0, 2)
                def _(turn_id):
                    side = jnp.where(odd_pair == 1, turn_id, 1 - turn_id)
                    target = e + (2 * side - 1) * reach

                    @pl.when(target < slabs)
                    def _():
                        def put(k, product):
                            state_out[side, k] = product

                        for half in by_halves(side, state_x[...], put):
                            send(
                                state_out.at[side, half],
                                state_in.at[level, 1 - side, half],
                                up_send.at[side],
                                reduce_recv.at[level, 1 - side],
                                (target + 1, c),
                            )

        @pl.when(row_role)
        def _():
            for index in (BENEATH_R, ABOVE_R):
                arrived(row_raw.at[index], mat_recv.at[index])
                row_w[index] = stacked(row_raw[index])
            arrived(rhs_row, rhs_recv)
            arrived(row_in.at[0, 1, pl.ds(0, parts - 1)], reduce_recv.at[0, 1])
            arrived(row_in.at[0, 0], reduce_recv.at[0, 0])
            row_x[...] = rhs_row[...] - row_in[0, 1] - row_in[0, 0]

            for j in range(1, ROW_LEVELS):
                @pl.when(level > j)
                def _():
                    arrived(row_in.at[j, 1], reduce_recv.at[j, 1])
                    arrived(row_in.at[j, 0], reduce_recv.at[j, 0])
                    row_x[...] -= row_in[j, 1] + row_in[j, 0]

            row_tall = split_tall(side_by_side(row_x[...]))

            @pl.loop(0, 2)
            def _(turn_id):
                side = jnp.where(odd_pair == 1, turn_id, 1 - turn_id)
                target = e + (2 * side - 1) * reach

                @pl.when(target < slabs)
                def _():
                    row_out[side] = join(times_rows(row_tall, row_w[side]))
                    target_level, _ = place_of(target, levels)
                    send_rows(
                        row_out.at[side],
                        target + 1,
                        target_level > ROW_LEVELS,
                        level,
                        1 - side,
                        up_send.at[side],
                    )

                @pl.when(turn_id == 0)
                def _():
                    sent_up(side)

            let_go()

        def send_solved(j, side, half):
            target = s + (2 * side - 1) * jnp.left_shift(jnp.int32(1), j)
            send(
                solved.at[half], solve_in.at[1 - side, half], solve_send.at[j, side],
                solve_recv.at[1 - side], (target, c),
            )

        def send_tier(j, half):
            send_solved(j, 1, half)

            @pl.when(not_root)
            def _():
                send_solved(j, 0, half)

        def first_tier(half):
            @pl.when(level > 1)
            def _():
                send_tier(level - 1, half)

        def put_solved(k, product):
            solved[k] = product

        def take_off(k, product):
            solved[k] -= product

        @pl.when(is_root)
        def _():
            convert(PIVOT)
            for half in by_halves(PIVOT, state_x[...], put_solved):
                first_tier(half)

        @pl.when(not_root)
        def _():
            @pl.when(state_role)
            def _():
                around(
                    s,
                    lambda device: send(
                        state_x, row_x.at[:, states_of(c)], gather_send, gather_recv, device
                    ),
                    skip_own=True,
                )
                row_x[:, states_of(c)] = state_x[...]
                arrived(psi_full.at[pl.ds(0, parts - 1)], gather_recv)

            arrived(row_raw.at[PIVOT], mat_recv.at[PIVOT])
            row_w[PIVOT] = stacked(row_raw[PIVOT])
            pivot_rows[...] = join(
                times_rows(split_tall(side_by_side(row_x[...])), row_w[PIVOT])
            )
            around(
                s,
                lambda device: send(
                    pivot_rows.at[states_of(device[1])], solved.at[c], part_send, part_recv, device
                ),
                skip_own=True,
            )
            solved[c] = pivot_rows[states_of(c)]
            convert_pair(BENEATH_S)
            arrived(rhs_state.at[pl.ds(0, parts - 1)], part_recv)

            early = jnp.where(jnp.logical_or(odd_pair == 1, jnp.logical_not(has_above)), 1, 0)
            last = 1 - early

            @pl.when(jnp.logical_or(early == 0, has_above))
            def _():
                arrived(solve_in.at[early], solve_recv.at[early])
                for _ in by_halves(BENEATH_S + early, solve_in[early], take_off):
                    pass

            arrived(solve_in.at[last], solve_recv.at[last])
            for half in by_halves(BENEATH_S + last, solve_in[last], take_off):
                first_tier(half)

        @pl.loop(1, level - 1)
        def _(i):
            send_tier(level - 1 - i, pl.ds(0, parts))

        @pl.when(not_root)
        def _():
            around(
                s - 2,
                lambda device: send(
                    solved, odd_in.at[1, :, states_of(c)], last_send.at[1], last_recv.at[1], device
                ),
            )

        around(
            s,
            lambda device: send(
                solved, odd_in.at[0, :, states_of(c)], last_send.at[0], last_recv.at[0], device
            ),
            skip_own=True,
        )
        odd_in[0, :, states_of(c)] = solved[...]
        around(
            s - 1,
            lambda device: send(
                solved.at[device[1]], out_in.at[states_of(c)], out_send, out_recv, device
            ),
        )

        def settle(side):
            def take():
                if side == 0:
                    arrived(solved_three, last_recv.at[0])
                else:
                    arrived(odd_in.at[1], last_recv.at[1])
                pivot_odd[...] -= join(
                    times_rows(split_tall(side_by_side(odd_in[side])), own_w[BENEATH_S + side])
                )

            if side == 0:
                take()
            else:
                pl.when(has_next)(take)

        solved_three = psi_full.at[pl.ds(0, parts - 1)]

        @pl.when(chip % 2 == 1)
        def _():
            settle(1)
            settle(0)

        @pl.when(chip % 2 == 0)
        def _():
            settle(0)
            settle(1)

        out[0] = pivot_odd[...].T

        arrived(psi_full.at[pl.ds(0, parts - 1)], psi_send)
        arrived(x_full.at[pl.ds(0, parts - 1)], x_send)
        arrived(up_in, serve_send)

        @pl.when(chip % 2 == 1)
        def _():
            sent_above()

        @pl.when(chip % 2 == 0)
        def _():
            sent_beneath()

        @pl.when(has_next)
        def _():
            arrived(tunnel_in, next_send)
            arrived(prev_parts, prev_send)

        @pl.when(not_root)
        def _():
            @pl.loop(0, 2)
            def _(side):
                @pl.when(jnp.logical_or(state_role, side == odd_pair))
                def _():
                    sent_up(side)

            arrived(rhs_row, last_send.at[1])

        arrived(psi_full.at[pl.ds(0, parts - 1)], last_send.at[0])
        arrived(rhs_state, out_send)

        @pl.when(not_root)
        def _():
            arrived(rhs_state.at[pl.ds(0, parts - 1)], part_send)

            @pl.when(state_role)
            def _():
                arrived(psi_full.at[pl.ds(0, parts - 1)], gather_send)

        @pl.loop(1, level)
        def _(j):
            arrived(solved, solve_send.at[j, 1])

            @pl.when(not_root)
            def _():
                arrived(solved, solve_send.at[j, 0])


def per_device(*args):
    slabs = lax.axis_size("slab")
    levels = slabs.bit_length() - 1
    parts = lax.axis_size("col")
    psi = args[0]
    rows, width = psi.shape[1:]
    depth = parts * rows
    quarter = width // parts
    f32, bf16 = jnp.float32, jnp.bfloat16

    def whole(*lead):
        return pltpu.VMEM((*lead, parts, width, rows), f32)

    def piece(*lead):
        return pltpu.VMEM((*lead, parts, quarter, rows), f32)

    dma = pltpu.SemaphoreType.DMA
    return pl.pallas_call(
        functools.partial(kernel, slabs, levels, parts),
        out_shape=jax.ShapeDtypeStruct(psi.shape, psi.dtype),
        in_specs=[pl.BlockSpec(memory_space=pl.ANY)] * len(args),
        out_specs=pl.BlockSpec(memory_space=pltpu.VMEM),
        scratch_shapes=[
            pltpu.VMEM((rows, width), f32),
            pltpu.VMEM((rows, depth), f32),
            pltpu.VMEM((rows, depth), f32),
            pltpu.VMEM((5, 2, rows, depth), f32),
            pltpu.VMEM((5, 2, depth, rows), f32),
            whole(),
            pltpu.VMEM((rows, depth), f32),
            pltpu.VMEM((width, rows), f32),
            pltpu.VMEM((width, rows), f32),
            whole(),
            whole(),
            whole(),
            pltpu.VMEM((2 * rows, depth), bf16),
            pltpu.VMEM((2 * rows, depth), bf16),
            pltpu.VMEM((5, 4 * rows, depth), bf16),
            pltpu.VMEM((3, 2, rows, depth), f32),
            pltpu.VMEM((3, 4 * rows, depth), bf16),
            pltpu.VMEM((5, parts, 2, depth, rows), f32),
            pltpu.VMEM((5, 2, depth, 2 * depth), bf16),
            pltpu.VMEM((width, rows), f32),
            pltpu.VMEM((2, width, rows), f32),
            whole(),
            whole(ROW_LEVELS, 2),
            whole(),
            pltpu.VMEM((2, width, rows), f32),
            piece(),
            piece(levels, 2),
            piece(),
            piece(2),
            piece(2),
            piece(),
            whole(2),
            pltpu.VMEM((width, rows), f32),
            pltpu.VMEM((width, rows), f32),
            dma((8,)),
            *[dma] * 10,
            dma((5,)),
            dma((5,)),
            dma((2,)),
            dma((2,)),
            dma((levels, 2)),
            dma((levels, 2)),
            dma((2,)),
            dma((2,)),
            dma((2,)),
            dma,
            dma,
            *[dma] * 6,
            pltpu.SemaphoreType.REGULAR,
        ],
        compiler_params=pltpu.CompilerParams(
            collective_id=0, has_side_effects=True, vmem_limit_bytes=56 * 2**20
        ),
    )(*args)


def solution(mesh):
    vector = P("slab", "col", None)
    block = P("slab", None, "col", None)
    return jax.shard_map(
        per_device,
        mesh=mesh,
        in_specs=(vector,) * 3 + (block,) * 5,
        out_specs=vector,
        check_vma=False,
    )
```

```python
import functools

import jax
import jax.numpy as jnp
from jax import lax
from jax.experimental import pallas as pl
from jax.experimental.pallas import tpu as pltpu
from jax.sharding import PartitionSpec as P

MESH = pl.DeviceIdType.MESH
half_step = 0.5
ROW_LEVELS = 2
BENEATH_R, ABOVE_R, PIVOT, BENEATH_S, ABOVE_S = range(5)


def rotate(values):
    height = values.shape[0]
    row = lax.broadcasted_iota(jnp.int32, values.shape, 0)
    return jnp.where(
        row % 2 == 0, -pltpu.roll(values, height - 1, 0), pltpu.roll(values, 1, 0)
    )


def split(values):
    high = values.astype(jnp.bfloat16)
    low = (values - high.astype(jnp.float32)).astype(jnp.bfloat16)
    return high, low


def split_tall(values):
    return jnp.concatenate(split(values), axis=0)


def fold(product):
    m, n = product.shape[0] // 2, product.shape[1] // 2
    return product[:m, :n] + (product[m:, :n] + product[:m, n:])


def times_rows(tall, block_rows):
    return fold(
        lax.dot_general(
            tall, block_rows, (((1,), (1,)), ((), ())), preferred_element_type=jnp.float32
        )
    )


def times_columns(tall, block_columns):
    return fold(jnp.dot(tall, block_columns, preferred_element_type=jnp.float32))


def join(both):
    n = both.shape[1] // 2
    return both[:, :n] + rotate(both[:, n:])


def side_by_side(pieces):
    return jnp.concatenate([pieces[k] for k in range(pieces.shape[0])], axis=1)


def place_of(slab, levels):
    level, reach = jnp.int32(0), jnp.int32(1)
    for k in range(1, levels + 1):
        at_least = slab % (2**k) == 0
        level = jnp.where(at_least, k, level)
        reach = jnp.where(at_least, 2**k, reach)
    return level, reach


def kernel(slabs, levels, parts, *refs):
    (
        psi_h, energy_h, tunnel_h, pivot_h, beneath_reduce_h, above_reduce_h,
        beneath_solve_h, above_solve_h, out,
        psi_raw, energy_v, tunnel_v, blocks_v, turned_v,
        psi_full, tunnel_in, up_rows, up_in, prev_parts, prev_send_v, x_full,
        energy_w, tunnel_w, own_w, row_raw, row_w, state_raw, state_w,
        pivot_odd, odd_out,
        rhs_row, row_in, row_x, row_out,
        rhs_state, state_in, state_x, state_out,
        solve_in, solved, odd_in, out_in, pivot_rows,
        load_sem, psi_send, psi_recv, next_send, next_recv, prev_send, prev_recv,
        x_send, x_recv, rhs_send, rhs_recv, mat_send, mat_recv, odd_send, up_send,
        reduce_recv, solve_send, solve_recv, last_send, last_recv, out_send, out_recv,
        gather_send, gather_recv, part_send, part_recv, serve_send, serve_recv, go,
    ) = refs
    s = lax.axis_index("slab")
    c = lax.axis_index("col")
    odd = s % 2 == 1
    even = s % 2 == 0
    chip = s // 2
    e = chip * 2
    level, reach = place_of(e, levels)
    level_next, _ = place_of(e + 2, levels)
    is_root = e == 0
    not_root = e > 0
    has_above = e + reach < slabs
    state_role = level > ROW_LEVELS
    row_role = level <= ROW_LEVELS
    has_next = e + 2 < slabs
    rows, width = psi_h.shape[1:]
    depth = parts * rows
    quarter = width // parts

    def around(slab, act, skip_own=False):
        for step in (2, 1, 3) if skip_own else (2, 1, 3, 0):
            act((slab, (c + step) % parts))

    def arrived(ref, sem):
        pltpu.make_async_copy(ref, ref, sem).wait()

    def send(source, target, send_sem, recv_sem, device):
        pltpu.make_async_remote_copy(
            src_ref=source, dst_ref=target, send_sem=send_sem, recv_sem=recv_sem,
            device_id=device, device_id_type=MESH,
        ).start()

    def states_of(col):
        return pl.ds(pl.multiple_of(col * quarter, quarter), quarter)

    def load(index, source, target):
        return pltpu.make_async_copy(source, target, load_sem.at[index])

    loads = [
        load(0, psi_h.at[0], psi_raw),
        load(1, tunnel_h.at[0], tunnel_v),
        load(2, energy_h.at[0], energy_v),
        load(3, beneath_reduce_h.at[0], blocks_v.at[BENEATH_R]),
        load(4, above_reduce_h.at[0], blocks_v.at[ABOVE_R]),
        load(5, pivot_h.at[0], blocks_v.at[PIVOT]),
        load(6, beneath_solve_h.at[0], blocks_v.at[BENEATH_S]),
        load(7, above_solve_h.at[0], blocks_v.at[ABOVE_S]),
    ]
    for copy in loads[:3]:
        copy.start()

    barrier = pltpu.get_barrier_semaphore()

    def greet(device):
        pl.semaphore_signal(barrier, inc=1, device_id=device, device_id_type=MESH)

    expected = jnp.int32(2 * parts - 1)

    @pl.when(jnp.logical_and(even, not_root))
    def _():
        around(s - 1, greet)

    @pl.when(jnp.logical_and(odd, has_next))
    def _():
        around(s + 1, greet)

    expected += parts * jnp.where(odd, has_next, not_root).astype(jnp.int32)
    around(s + 1 - 2 * (s % 2), greet)
    around(s, greet, skip_own=True)
    for j in range(1, levels):
        for sign in (-1, 1):
            target = s + sign * 2**j
            there = jnp.logical_and(target >= 0, target < slabs)
            if j > 1:
                there = jnp.logical_and(there, j <= level)
            there = jnp.logical_and(there, odd)
            count = parts if j <= max(ROW_LEVELS, 1) else 1
            expected += count * there.astype(jnp.int32)

            @pl.when(there)
            def _():
                if count > 1:
                    around(target, greet)
                else:
                    greet((target, c))

    for copy in loads[3:]:
        copy.start()

    loads[0].wait()
    own = psi_raw[...].T
    psi_full[c] = own
    loads[1].wait()

    pl.semaphore_wait(barrier, expected)

    def make_prev():
        wide_tunnel = jnp.concatenate(split(tunnel_v[...]), axis=1)
        partial = times_columns(split_tall(own), wide_tunnel)
        for k in range(parts):
            prev_send_v[k] = partial[:, k * rows : (k + 1) * rows]

    def send_psi_row():
        around(
            s,
            lambda device: send(psi_full.at[c], psi_full.at[c], psi_send, psi_recv, device),
            skip_own=True,
        )

    def send_prev():
        around(
            s + 1,
            lambda device: send(
                prev_send_v.at[device[1]], prev_parts.at[c], prev_send, prev_recv, device
            ),
        )

    def send_tunnel():
        send(tunnel_v, tunnel_in, next_send, next_recv, (s + 1, c))

    @pl.when(odd)
    def _():
        @pl.when(has_next)
        def _():
            send_tunnel()

        send_psi_row()
        make_prev()

    @pl.when(even)
    def _():
        send_psi_row()
        make_prev()
        send_prev()
        send_tunnel()

    def stacked(block):
        return split_tall(block.reshape(2 * rows, depth))

    loads[2].wait()
    energy_w[...] = split_tall(energy_v[...])
    for index in range(5):
        loads[3 + index].wait()

    def turn(index):
        for part in range(2):
            turned_v[index, part] = blocks_v[index, part].T

    def pass_on(index):
        around(
            s + 1,
            lambda device: send(
                turned_v.at[index],
                state_raw.at[index, c],
                mat_send.at[index],
                mat_recv.at[index],
                device,
            ),
        )

    def hand_over(index):
        send(
            blocks_v.at[index], row_raw.at[index], mat_send.at[index], mat_recv.at[index],
            (s + 1, c),
        )

    @pl.when(even)
    def _():
        @pl.when(is_root)
        def _():
            turn(PIVOT)
            pass_on(PIVOT)

        @pl.when(not_root)
        def _():
            hand_over(PIVOT)

            @pl.when(row_role)
            def _():
                hand_over(BENEATH_R)
                hand_over(ABOVE_R)

            @pl.when(state_role)
            def _():
                turn(BENEATH_R)
                pass_on(BENEATH_R)

                @pl.when(has_above)
                def _():
                    turn(ABOVE_R)
                    pass_on(ABOVE_R)

    @pl.when(odd)
    def _():
        own_w[BENEATH_R] = stacked(blocks_v[BENEATH_R])
        own_w[ABOVE_R] = stacked(blocks_v[ABOVE_R])

    arrived(psi_full.at[pl.ds(0, parts - 1)], psi_recv)
    psi_tall = split_tall(side_by_side(psi_full[...]))

    def serve_beneath():
        arrived(tunnel_in, next_recv)
        tunnel_w[...] = split_tall(tunnel_in[...])
        up_rows[...] = times_rows(psi_tall, tunnel_w[...])
        send(up_rows, up_in, serve_send, serve_recv, (s - 1, c))

    @pl.when(jnp.logical_and(even, not_root))
    def _():
        serve_beneath()

    x_full[c] = times_rows(psi_tall, energy_w[...])

    @pl.when(s > 0)
    def _():
        arrived(prev_parts, prev_recv)
        x_full[c] += (prev_parts[0] + prev_parts[1]) + (prev_parts[2] + prev_parts[3])

    @pl.when(s + 1 < slabs)
    def _():
        arrived(up_in, serve_recv)
        x_full[c] += up_in[...]

    x_full[c] = psi_full[c] - half_step * rotate(x_full[c])

    @pl.when(even)
    def _():
        @pl.when(state_role)
        def _():
            around(
                s + 1,
                lambda device: send(
                    x_full.at[c, states_of(device[1])], rhs_state.at[c], rhs_send, rhs_recv, device
                ),
            )

        @pl.when(row_role)
        def _():
            around(
                s + 1,
                lambda device: send(x_full.at[c], rhs_row.at[c], rhs_send, rhs_recv, device),
            )

        @pl.when(not_root)
        def _():
            turn(BENEATH_S)
            turn(ABOVE_S)

        pl.semaphore_wait(go, 1)

        @pl.when(not_root)
        def _():
            pass_on(BENEATH_S)

            @pl.when(has_above)
            def _():
                pass_on(ABOVE_S)

        arrived(out_in, out_recv)
        out[0] = out_in[...].T

        arrived(psi_full.at[pl.ds(0, parts - 1)], psi_send)
        arrived(prev_parts, prev_send)
        arrived(tunnel_in, next_send)

        @pl.when(not_root)
        def _():
            arrived(up_in, serve_send)
            arrived(state_raw.at[BENEATH_S], mat_send.at[BENEATH_S])
            arrived(row_raw.at[PIVOT], mat_send.at[PIVOT])

            @pl.when(has_above)
            def _():
                arrived(state_raw.at[ABOVE_S], mat_send.at[ABOVE_S])

            @pl.when(state_role)
            def _():
                arrived(state_raw.at[BENEATH_R], mat_send.at[BENEATH_R])

                @pl.when(has_above)
                def _():
                    arrived(state_raw.at[ABOVE_R], mat_send.at[ABOVE_R])

            @pl.when(row_role)
            def _():
                arrived(row_raw.at[BENEATH_R], mat_send.at[BENEATH_R])
                arrived(row_raw.at[ABOVE_R], mat_send.at[ABOVE_R])

        @pl.when(is_root)
        def _():
            arrived(state_raw.at[PIVOT], mat_send.at[PIVOT])

        @pl.when(state_role)
        def _():
            arrived(rhs_state, rhs_send)

        @pl.when(row_role)
        def _():
            arrived(rhs_row, rhs_send)

    @pl.when(odd)
    def _():
        around(
            s,
            lambda device: send(x_full.at[c], x_full.at[c], x_send, x_recv, device),
            skip_own=True,
        )
        serve_beneath()

        @pl.when(has_next)
        def _():
            send_prev()

        own_w[PIVOT] = stacked(blocks_v[PIVOT])
        own_w[BENEATH_S] = stacked(blocks_v[BENEATH_S])
        own_w[ABOVE_S] = stacked(blocks_v[ABOVE_S])

        arrived(x_full.at[pl.ds(0, parts - 1)], x_recv)
        tall = split_tall(side_by_side(x_full[...]))

        def send_rows(source, host, to_state, tier, side, sem, skip_own=False):
            @pl.when(to_state)
            def _():
                around(
                    host,
                    lambda device: send(
                        source.at[states_of(device[1])],
                        state_in.at[tier, side, c],
                        sem,
                        reduce_recv.at[tier, side],
                        device,
                    ),
                    skip_own,
                )

            @pl.when(jnp.logical_not(to_state))
            def _():
                around(
                    host,
                    lambda device: send(
                        source,
                        row_in.at[jnp.minimum(tier, ROW_LEVELS - 1), side, c],
                        sem,
                        reduce_recv.at[tier, side],
                        device,
                    ),
                    skip_own,
                )

        def odd_beneath():
            odd_out[0] = join(times_rows(tall, own_w[BENEATH_R]))
            send_rows(odd_out.at[0], s, state_role, 0, 1, odd_send.at[0], skip_own=True)

            @pl.when(state_role)
            def _():
                state_in[0, 1, c] = odd_out[0, states_of(c)]

            @pl.when(row_role)
            def _():
                row_in[0, 1, c] = odd_out[0]

        def odd_above():
            @pl.when(has_next)
            def _():
                odd_out[1] = join(times_rows(tall, own_w[ABOVE_R]))
                send_rows(
                    odd_out.at[1], s + 2, level_next > ROW_LEVELS, 0, 0, odd_send.at[1]
                )

        def sent_beneath():
            @pl.when(state_role)
            def _():
                arrived(rhs_state.at[pl.ds(0, parts - 1)], odd_send.at[0])

            @pl.when(row_role)
            def _():
                arrived(rhs_row.at[pl.ds(0, parts - 1)], odd_send.at[0])

        def sent_above():
            @pl.when(jnp.logical_and(has_next, level_next > ROW_LEVELS))
            def _():
                arrived(rhs_state, odd_send.at[1])

            @pl.when(jnp.logical_and(has_next, level_next <= ROW_LEVELS))
            def _():
                arrived(rhs_row, odd_send.at[1])

        @pl.when(chip % 2 == 1)
        def _():
            odd_beneath()
            sent_beneath()
            odd_above()

        @pl.when(chip % 2 == 0)
        def _():
            odd_above()
            sent_above()
            odd_beneath()

        def sent_up(side):
            target = e + (2 * side - 1) * reach
            target_level, _ = place_of(target, levels)
            small = target_level > ROW_LEVELS

            @pl.when(jnp.logical_and(target < slabs, small))
            def _():
                arrived(rhs_state, up_send.at[side])

            @pl.when(jnp.logical_and(target < slabs, jnp.logical_not(small)))
            def _():
                arrived(rhs_row, up_send.at[side])

        def let_go():
            pl.semaphore_signal(go, inc=1, device_id=(s - 1, c), device_id_type=MESH)

        @pl.when(state_role)
        def _():
            let_go()

        pivot_odd[...] = join(times_rows(tall, own_w[PIVOT]))

        odd_pair = (e // reach // 2) % 2

        pieces = parts // 2

        def convert(index):
            arrived(state_raw.at[index], mat_recv.at[index])
            for part in range(2):
                for k in range(parts):
                    half, place = k // pieces, k % pieces
                    at = (part * pieces + place) * rows
                    high, low = split(state_raw[index, k, part])
                    state_w[index, half, :, at : at + rows] = high
                    state_w[index, half, :, depth + at : depth + at + rows] = low

        def convert_pair(first):
            @pl.loop(first, first + 1 + has_above.astype(jnp.int32))
            def _(index):
                convert(index)

        def by_halves(index, vectors, take):
            tall = split_tall(side_by_side(vectors))
            for half in range(2):
                product = join(times_columns(tall, state_w[index, half]))
                for place in range(pieces):
                    take(half * pieces + place, product[:, place * rows : (place + 1) * rows])
                yield pl.ds(half * pieces, pieces)

        @pl.when(state_role)
        def _():
            @pl.when(not_root)
            def _():
                convert_pair(BENEATH_R)

            arrived(rhs_state, rhs_recv)
            arrived(state_in.at[0, 1, pl.ds(0, parts - 1)], reduce_recv.at[0, 1])
            state_x[...] = rhs_state[...] - state_in[0, 1]

            @pl.when(not_root)
            def _():
                arrived(state_in.at[0, 0], reduce_recv.at[0, 0])
                state_x[...] -= state_in[0, 0]

            @pl.loop(1, level)
            def _(j):
                arrived(state_in.at[j, 1], reduce_recv.at[j, 1])
                state_x[...] -= state_in[j, 1]

                @pl.when(not_root)
                def _():
                    arrived(state_in.at[j, 0], reduce_recv.at[j, 0])
                    state_x[...] -= state_in[j, 0]

            @pl.when(not_root)
            def _():
                @pl.loop(0, 2)
                def _(turn_id):
                    side = jnp.where(odd_pair == 1, turn_id, 1 - turn_id)
                    target = e + (2 * side - 1) * reach

                    @pl.when(target < slabs)
                    def _():
                        def put(k, product):
                            state_out[side, k] = product

                        for half in by_halves(side, state_x[...], put):
                            send(
                                state_out.at[side, half],
                                state_in.at[level, 1 - side, half],
                                up_send.at[side],
                                reduce_recv.at[level, 1 - side],
                                (target + 1, c),
                            )

        @pl.when(row_role)
        def _():
            for index in (BENEATH_R, ABOVE_R):
                arrived(row_raw.at[index], mat_recv.at[index])
                row_w[index] = stacked(row_raw[index])
            arrived(rhs_row, rhs_recv)
            arrived(row_in.at[0, 1, pl.ds(0, parts - 1)], reduce_recv.at[0, 1])
            arrived(row_in.at[0, 0], reduce_recv.at[0, 0])
            row_x[...] = rhs_row[...] - row_in[0, 1] - row_in[0, 0]

            for j in range(1, ROW_LEVELS):
                @pl.when(level > j)
                def _():
                    arrived(row_in.at[j, 1], reduce_recv.at[j, 1])
                    arrived(row_in.at[j, 0], reduce_recv.at[j, 0])
                    row_x[...] -= row_in[j, 1] + row_in[j, 0]

            row_tall = split_tall(side_by_side(row_x[...]))

            @pl.loop(0, 2)
            def _(turn_id):
                side = jnp.where(odd_pair == 1, turn_id, 1 - turn_id)
                target = e + (2 * side - 1) * reach

                @pl.when(target < slabs)
                def _():
                    row_out[side] = join(times_rows(row_tall, row_w[side]))
                    target_level, _ = place_of(target, levels)
                    send_rows(
                        row_out.at[side],
                        target + 1,
                        target_level > ROW_LEVELS,
                        level,
                        1 - side,
                        up_send.at[side],
                    )

                @pl.when(turn_id == 0)
                def _():
                    sent_up(side)

            let_go()

        def send_solved(j, side, half):
            target = s + (2 * side - 1) * jnp.left_shift(jnp.int32(1), j)
            send(
                solved.at[half], solve_in.at[1 - side, half], solve_send.at[j, side],
                solve_recv.at[1 - side], (target, c),
            )

        def send_tier(j, half):
            send_solved(j, 1, half)

            @pl.when(not_root)
            def _():
                send_solved(j, 0, half)

        def first_tier(half):
            @pl.when(level > 1)
            def _():
                send_tier(level - 1, half)

        def put_solved(k, product):
            solved[k] = product

        def take_off(k, product):
            solved[k] -= product

        @pl.when(is_root)
        def _():
            convert(PIVOT)
            for half in by_halves(PIVOT, state_x[...], put_solved):
                first_tier(half)

        @pl.when(not_root)
        def _():
            @pl.when(state_role)
            def _():
                around(
                    s,
                    lambda device: send(
                        state_x, row_x.at[:, states_of(c)], gather_send, gather_recv, device
                    ),
                    skip_own=True,
                )
                row_x[:, states_of(c)] = state_x[...]
                arrived(psi_full.at[pl.ds(0, parts - 1)], gather_recv)

            arrived(row_raw.at[PIVOT], mat_recv.at[PIVOT])
            row_w[PIVOT] = stacked(row_raw[PIVOT])
            pivot_rows[...] = join(
                times_rows(split_tall(side_by_side(row_x[...])), row_w[PIVOT])
            )
            around(
                s,
                lambda device: send(
                    pivot_rows.at[states_of(device[1])], solved.at[c], part_send, part_recv, device
                ),
                skip_own=True,
            )
            solved[c] = pivot_rows[states_of(c)]
            convert_pair(BENEATH_S)
            arrived(rhs_state.at[pl.ds(0, parts - 1)], part_recv)

            early = jnp.where(jnp.logical_or(odd_pair == 1, jnp.logical_not(has_above)), 1, 0)
            last = 1 - early

            @pl.when(jnp.logical_or(early == 0, has_above))
            def _():
                arrived(solve_in.at[early], solve_recv.at[early])
                for _ in by_halves(BENEATH_S + early, solve_in[early], take_off):
                    pass

            arrived(solve_in.at[last], solve_recv.at[last])
            for half in by_halves(BENEATH_S + last, solve_in[last], take_off):
                first_tier(half)

        @pl.loop(1, level - 1)
        def _(i):
            send_tier(level - 1 - i, pl.ds(0, parts))

        @pl.when(not_root)
        def _():
            around(
                s - 2,
                lambda device: send(
                    solved, odd_in.at[1, :, states_of(c)], last_send.at[1], last_recv.at[1], device
                ),
            )

        around(
            s,
            lambda device: send(
                solved, odd_in.at[0, :, states_of(c)], last_send.at[0], last_recv.at[0], device
            ),
            skip_own=True,
        )
        odd_in[0, :, states_of(c)] = solved[...]
        around(
            s - 1,
            lambda device: send(
                solved.at[device[1]], out_in.at[states_of(c)], out_send, out_recv, device
            ),
        )

        def settle(side):
            def take():
                if side == 0:
                    arrived(solved_three, last_recv.at[0])
                else:
                    arrived(odd_in.at[1], last_recv.at[1])
                pivot_odd[...] -= join(
                    times_rows(split_tall(side_by_side(odd_in[side])), own_w[BENEATH_S + side])
                )

            if side == 0:
                take()
            else:
                pl.when(has_next)(take)

        solved_three = psi_full.at[pl.ds(0, parts - 1)]

        @pl.when(chip % 2 == 1)
        def _():
            settle(1)
            settle(0)

        @pl.when(chip % 2 == 0)
        def _():
            settle(0)
            settle(1)

        out[0] = pivot_odd[...].T

        arrived(psi_full.at[pl.ds(0, parts - 1)], psi_send)
        arrived(x_full.at[pl.ds(0, parts - 1)], x_send)
        arrived(up_in, serve_send)

        @pl.when(chip % 2 == 1)
        def _():
            sent_above()

        @pl.when(chip % 2 == 0)
        def _():
            sent_beneath()

        @pl.when(has_next)
        def _():
            arrived(tunnel_in, next_send)
            arrived(prev_parts, prev_send)

        @pl.when(not_root)
        def _():
            @pl.loop(0, 2)
            def _(side):
                @pl.when(jnp.logical_or(state_role, side == odd_pair))
                def _():
                    sent_up(side)

            arrived(rhs_row, last_send.at[1])

        arrived(psi_full.at[pl.ds(0, parts - 1)], last_send.at[0])
        arrived(rhs_state, out_send)

        @pl.when(not_root)
        def _():
            arrived(rhs_state.at[pl.ds(0, parts - 1)], part_send)

            @pl.when(state_role)
            def _():
                arrived(psi_full.at[pl.ds(0, parts - 1)], gather_send)

        @pl.loop(1, level)
        def _(j):
            arrived(solved, solve_send.at[j, 1])

            @pl.when(not_root)
            def _():
                arrived(solved, solve_send.at[j, 0])


def per_device(*args):
    slabs = lax.axis_size("slab")
    levels = slabs.bit_length() - 1
    parts = lax.axis_size("col")
    psi = args[0]
    rows, width = psi.shape[1:]
    depth = parts * rows
    quarter = width // parts
    f32, bf16 = jnp.float32, jnp.bfloat16

    def whole(*lead):
        return pltpu.VMEM((*lead, parts, width, rows), f32)

    def piece(*lead):
        return pltpu.VMEM((*lead, parts, quarter, rows), f32)

    dma = pltpu.SemaphoreType.DMA
    return pl.pallas_call(
        functools.partial(kernel, slabs, levels, parts),
        out_shape=jax.ShapeDtypeStruct(psi.shape, psi.dtype),
        in_specs=[pl.BlockSpec(memory_space=pl.ANY)] * len(args),
        out_specs=pl.BlockSpec(memory_space=pltpu.VMEM),
        scratch_shapes=[
            pltpu.VMEM((rows, width), f32),
            pltpu.VMEM((rows, depth), f32),
            pltpu.VMEM((rows, depth), f32),
            pltpu.VMEM((5, 2, rows, depth), f32),
            pltpu.VMEM((5, 2, depth, rows), f32),
            whole(),
            pltpu.VMEM((rows, depth), f32),
            pltpu.VMEM((width, rows), f32),
            pltpu.VMEM((width, rows), f32),
            whole(),
            whole(),
            whole(),
            pltpu.VMEM((2 * rows, depth), bf16),
            pltpu.VMEM((2 * rows, depth), bf16),
            pltpu.VMEM((5, 4 * rows, depth), bf16),
            pltpu.VMEM((3, 2, rows, depth), f32),
            pltpu.VMEM((3, 4 * rows, depth), bf16),
            pltpu.VMEM((5, parts, 2, depth, rows), f32),
            pltpu.VMEM((5, 2, depth, 2 * depth), bf16),
            pltpu.VMEM((width, rows), f32),
            pltpu.VMEM((2, width, rows), f32),
            whole(),
            whole(ROW_LEVELS, 2),
            whole(),
            pltpu.VMEM((2, width, rows), f32),
            piece(),
            piece(levels, 2),
            piece(),
            piece(2),
            piece(2),
            piece(),
            whole(2),
            pltpu.VMEM((width, rows), f32),
            pltpu.VMEM((width, rows), f32),
            dma((8,)),
            *[dma] * 10,
            dma((5,)),
            dma((5,)),
            dma((2,)),
            dma((2,)),
            dma((levels, 2)),
            dma((levels, 2)),
            dma((2,)),
            dma((2,)),
            dma((2,)),
            dma,
            dma,
            *[dma] * 6,
            pltpu.SemaphoreType.REGULAR,
        ],
        compiler_params=pltpu.CompilerParams(
            collective_id=0, has_side_effects=True, vmem_limit_bytes=56 * 2**20
        ),
    )(*args)


def solution(mesh):
    vector = P("slab", "col", None)
    block = P("slab", None, "col", None)
    return jax.shard_map(
        per_device,
        mesh=mesh,
        in_specs=(vector,) * 3 + (block,) * 5,
        out_specs=vector,
        check_vma=False,
    )
```

```python
import functools

import jax
import jax.numpy as jnp
from jax import lax
from jax.experimental import pallas as pl
from jax.experimental.pallas import tpu as pltpu
from jax.sharding import PartitionSpec as P

MESH = pl.DeviceIdType.MESH
half_step = 0.5
ROW_LEVELS = 2
BENEATH_R, ABOVE_R, PIVOT, BENEATH_S, ABOVE_S = range(5)


def rotate(values):
    height = values.shape[0]
    row = lax.broadcasted_iota(jnp.int32, values.shape, 0)
    return jnp.where(
        row % 2 == 0, -pltpu.roll(values, height - 1, 0), pltpu.roll(values, 1, 0)
    )


def split(values):
    high = values.astype(jnp.bfloat16)
    low = (values - high.astype(jnp.float32)).astype(jnp.bfloat16)
    return high, low


def split_tall(values):
    return jnp.concatenate(split(values), axis=0)


def fold(product):
    m, n = product.shape[0] // 2, product.shape[1] // 2
    return product[:m, :n] + (product[m:, :n] + product[:m, n:])


def times_rows(tall, block_rows):
    return fold(
        lax.dot_general(
            tall, block_rows, (((1,), (1,)), ((), ())), preferred_element_type=jnp.float32
        )
    )


def times_columns(tall, block_columns):
    return fold(jnp.dot(tall, block_columns, preferred_element_type=jnp.float32))


def join(both):
    n = both.shape[1] // 2
    return both[:, :n] + rotate(both[:, n:])


def side_by_side(pieces):
    return jnp.concatenate([pieces[k] for k in range(pieces.shape[0])], axis=1)


def place_of(slab, levels):
    level, reach = jnp.int32(0), jnp.int32(1)
    for k in range(1, levels + 1):
        at_least = slab % (2**k) == 0
        level = jnp.where(at_least, k, level)
        reach = jnp.where(at_least, 2**k, reach)
    return level, reach


def kernel(slabs, levels, parts, *refs):
    (
        psi_h, energy_h, tunnel_h, pivot_h, beneath_reduce_h, above_reduce_h,
        beneath_solve_h, above_solve_h, out,
        psi_raw, energy_v, tunnel_v, blocks_v, turned_v,
        psi_full, tunnel_in, up_rows, up_in, prev_parts, prev_send_v, x_full,
        energy_w, tunnel_w, own_w, row_raw, row_w, state_raw, state_w,
        pivot_odd, odd_out,
        rhs_row, row_in, row_x, row_out,
        rhs_state, state_in, state_x, state_out,
        solve_in, solved, odd_in, out_in, pivot_rows,
        load_sem, psi_send, psi_recv, next_send, next_recv, prev_send, prev_recv,
        x_send, x_recv, rhs_send, rhs_recv, mat_send, mat_recv, odd_send, up_send,
        reduce_recv, solve_send, solve_recv, last_send, last_recv, out_send, out_recv,
        gather_send, gather_recv, part_send, part_recv, serve_send, serve_recv, go,
    ) = refs
    s = lax.axis_index("slab")
    c = lax.axis_index("col")
    odd = s % 2 == 1
    even = s % 2 == 0
    chip = s // 2
    e = chip * 2
    level, reach = place_of(e, levels)
    level_next, _ = place_of(e + 2, levels)
    is_root = e == 0
    not_root = e > 0
    has_above = e + reach < slabs
    odd_pair = (e // reach // 2) % 2
    state_role = level > ROW_LEVELS
    row_role = level <= ROW_LEVELS
    has_next = e + 2 < slabs
    rows, width = psi_h.shape[1:]
    depth = parts * rows
    quarter = width // parts

    def around(slab, act, skip_own=False):
        for step in (2, 1, 3) if skip_own else (2, 1, 3, 0):
            act((slab, (c + step) % parts))

    def arrived(ref, sem):
        pltpu.make_async_copy(ref, ref, sem).wait()

    def send(source, target, send_sem, recv_sem, device):
        pltpu.make_async_remote_copy(
            src_ref=source, dst_ref=target, send_sem=send_sem, recv_sem=recv_sem,
            device_id=device, device_id_type=MESH,
        ).start()

    def states_of(col):
        return pl.ds(pl.multiple_of(col * quarter, quarter), quarter)

    def load(index, source, target):
        return pltpu.make_async_copy(source, target, load_sem.at[index])

    loads = [
        load(0, psi_h.at[0], psi_raw),
        load(1, tunnel_h.at[0], tunnel_v),
        load(2, energy_h.at[0], energy_v),
        load(3, beneath_reduce_h.at[0], blocks_v.at[BENEATH_R]),
        load(4, above_reduce_h.at[0], blocks_v.at[ABOVE_R]),
        load(5, pivot_h.at[0], blocks_v.at[PIVOT]),
        load(6, beneath_solve_h.at[0], blocks_v.at[BENEATH_S]),
        load(7, above_solve_h.at[0], blocks_v.at[ABOVE_S]),
    ]
    for copy in loads[:3]:
        copy.start()

    barrier = pltpu.get_barrier_semaphore()

    def greet(device):
        pl.semaphore_signal(barrier, inc=1, device_id=device, device_id_type=MESH)

    expected = jnp.int32(2 * parts - 1)

    @pl.when(jnp.logical_and(even, not_root))
    def _():
        around(s - 1, greet)

    @pl.when(jnp.logical_and(odd, has_next))
    def _():
        around(s + 1, greet)

    expected += parts * jnp.where(odd, has_next, not_root).astype(jnp.int32)
    around(s + 1 - 2 * (s % 2), greet)
    around(s, greet, skip_own=True)
    for j in range(1, levels):
        for sign in (-1, 1):
            target = s + sign * 2**j
            there = jnp.logical_and(target >= 0, target < slabs)
            if j > 1:
                there = jnp.logical_and(there, j <= level)
            there = jnp.logical_and(there, odd)
            count = parts if j <= max(ROW_LEVELS, 1) else 1
            expected += count * there.astype(jnp.int32)

            @pl.when(there)
            def _():
                if count > 1:
                    around(target, greet)
                else:
                    greet((target, c))

    for copy in loads[3:]:
        copy.start()

    loads[0].wait()
    own = psi_raw[...].T
    psi_full[c] = own
    loads[1].wait()

    pl.semaphore_wait(barrier, expected)

    def make_prev():
        wide_tunnel = jnp.concatenate(split(tunnel_v[...]), axis=1)
        partial = times_columns(split_tall(own), wide_tunnel)
        for k in range(parts):
            prev_send_v[k] = partial[:, k * rows : (k + 1) * rows]

    def send_psi_row():
        around(
            s,
            lambda device: send(psi_full.at[c], psi_full.at[c], psi_send, psi_recv, device),
            skip_own=True,
        )

    def send_prev():
        around(
            s + 1,
            lambda device: send(
                prev_send_v.at[device[1]], prev_parts.at[c], prev_send, prev_recv, device
            ),
        )

    def send_tunnel():
        send(tunnel_v, tunnel_in, next_send, next_recv, (s + 1, c))

    @pl.when(odd)
    def _():
        send_psi_row()

        @pl.when(has_next)
        def _():
            send_tunnel()

        make_prev()

    @pl.when(even)
    def _():
        send_psi_row()
        make_prev()
        send_prev()
        send_tunnel()

    def stacked(block):
        return split_tall(block.reshape(2 * rows, depth))

    loads[2].wait()
    energy_w[...] = split_tall(energy_v[...])
    for index in range(5):
        loads[3 + index].wait()

    def turn(index):
        for part in range(2):
            turned_v[index, part] = blocks_v[index, part].T

    def pass_on(index):
        around(
            s + 1,
            lambda device: send(
                turned_v.at[index],
                state_raw.at[index, c],
                mat_send.at[index],
                mat_recv.at[index],
                device,
            ),
        )

    def hand_over(index):
        send(
            blocks_v.at[index], row_raw.at[index], mat_send.at[index], mat_recv.at[index],
            (s + 1, c),
        )

    @pl.when(even)
    def _():
        @pl.when(is_root)
        def _():
            turn(PIVOT)
            pass_on(PIVOT)

        @pl.when(not_root)
        def _():
            hand_over(PIVOT)

            @pl.when(row_role)
            def _():
                hand_over(BENEATH_R)
                hand_over(ABOVE_R)

            @pl.when(state_role)
            def _():
                @pl.loop(0, 2)
                def _(turn_id):
                    side = jnp.where(odd_pair == 1, turn_id, 1 - turn_id)

                    @pl.when(jnp.logical_or(side == 0, has_above))
                    def _():
                        turn(side)
                        pass_on(side)

    @pl.when(odd)
    def _():
        own_w[BENEATH_R] = stacked(blocks_v[BENEATH_R])
        own_w[ABOVE_R] = stacked(blocks_v[ABOVE_R])

    arrived(psi_full.at[pl.ds(0, parts - 1)], psi_recv)
    psi_tall = split_tall(side_by_side(psi_full[...]))

    def serve_beneath():
        arrived(tunnel_in, next_recv)
        tunnel_w[...] = split_tall(tunnel_in[...])
        up_rows[...] = times_rows(psi_tall, tunnel_w[...])
        send(up_rows, up_in, serve_send, serve_recv, (s - 1, c))

    @pl.when(jnp.logical_and(even, not_root))
    def _():
        serve_beneath()

    x_full[c] = times_rows(psi_tall, energy_w[...])

    @pl.when(s > 0)
    def _():
        arrived(prev_parts, prev_recv)
        x_full[c] += (prev_parts[0] + prev_parts[1]) + (prev_parts[2] + prev_parts[3])

    @pl.when(s + 1 < slabs)
    def _():
        arrived(up_in, serve_recv)
        x_full[c] += up_in[...]

    x_full[c] = psi_full[c] - half_step * rotate(x_full[c])

    @pl.when(even)
    def _():
        @pl.when(state_role)
        def _():
            around(
                s + 1,
                lambda device: send(
                    x_full.at[c, states_of(device[1])], rhs_state.at[c], rhs_send, rhs_recv, device
                ),
            )

        @pl.when(row_role)
        def _():
            around(
                s + 1,
                lambda device: send(x_full.at[c], rhs_row.at[c], rhs_send, rhs_recv, device),
            )

        @pl.when(not_root)
        def _():
            turn(BENEATH_S)
            turn(ABOVE_S)

        pl.semaphore_wait(go, 1)

        @pl.when(not_root)
        def _():
            pass_on(BENEATH_S)

            @pl.when(has_above)
            def _():
                pass_on(ABOVE_S)

        arrived(out_in, out_recv)
        out[0] = out_in[...].T

        arrived(psi_full.at[pl.ds(0, parts - 1)], psi_send)
        arrived(prev_parts, prev_send)
        arrived(tunnel_in, next_send)

        @pl.when(not_root)
        def _():
            arrived(up_in, serve_send)
            arrived(state_raw.at[BENEATH_S], mat_send.at[BENEATH_S])
            arrived(row_raw.at[PIVOT], mat_send.at[PIVOT])

            @pl.when(has_above)
            def _():
                arrived(state_raw.at[ABOVE_S], mat_send.at[ABOVE_S])

            @pl.when(state_role)
            def _():
                arrived(state_raw.at[BENEATH_R], mat_send.at[BENEATH_R])

                @pl.when(has_above)
                def _():
                    arrived(state_raw.at[ABOVE_R], mat_send.at[ABOVE_R])

            @pl.when(row_role)
            def _():
                arrived(row_raw.at[BENEATH_R], mat_send.at[BENEATH_R])
                arrived(row_raw.at[ABOVE_R], mat_send.at[ABOVE_R])

        @pl.when(is_root)
        def _():
            arrived(state_raw.at[PIVOT], mat_send.at[PIVOT])

        @pl.when(state_role)
        def _():
            arrived(rhs_state, rhs_send)

        @pl.when(row_role)
        def _():
            arrived(rhs_row, rhs_send)

    @pl.when(odd)
    def _():
        around(
            s,
            lambda device: send(x_full.at[c], x_full.at[c], x_send, x_recv, device),
            skip_own=True,
        )
        serve_beneath()

        @pl.when(has_next)
        def _():
            send_prev()

        own_w[PIVOT] = stacked(blocks_v[PIVOT])
        own_w[BENEATH_S] = stacked(blocks_v[BENEATH_S])
        own_w[ABOVE_S] = stacked(blocks_v[ABOVE_S])

        arrived(x_full.at[pl.ds(0, parts - 1)], x_recv)
        tall = split_tall(side_by_side(x_full[...]))

        def send_rows(source, host, to_state, tier, side, sem, skip_own=False):
            @pl.when(to_state)
            def _():
                around(
                    host,
                    lambda device: send(
                        source.at[states_of(device[1])],
                        state_in.at[tier, side, c],
                        sem,
                        reduce_recv.at[tier, side],
                        device,
                    ),
                    skip_own,
                )

            @pl.when(jnp.logical_not(to_state))
            def _():
                around(
                    host,
                    lambda device: send(
                        source,
                        row_in.at[jnp.minimum(tier, ROW_LEVELS - 1), side, c],
                        sem,
                        reduce_recv.at[tier, side],
                        device,
                    ),
                    skip_own,
                )

        def odd_beneath():
            odd_out[0] = join(times_rows(tall, own_w[BENEATH_R]))
            send_rows(odd_out.at[0], s, state_role, 0, 1, odd_send.at[0], skip_own=True)

            @pl.when(state_role)
            def _():
                state_in[0, 1, c] = odd_out[0, states_of(c)]

            @pl.when(row_role)
            def _():
                row_in[0, 1, c] = odd_out[0]

        def odd_above():
            @pl.when(has_next)
            def _():
                odd_out[1] = join(times_rows(tall, own_w[ABOVE_R]))
                send_rows(
                    odd_out.at[1], s + 2, level_next > ROW_LEVELS, 0, 0, odd_send.at[1]
                )

        def sent_beneath():
            @pl.when(state_role)
            def _():
                arrived(rhs_state.at[pl.ds(0, parts - 1)], odd_send.at[0])

            @pl.when(row_role)
            def _():
                arrived(rhs_row.at[pl.ds(0, parts - 1)], odd_send.at[0])

        def sent_above():
            @pl.when(jnp.logical_and(has_next, level_next > ROW_LEVELS))
            def _():
                arrived(rhs_state, odd_send.at[1])

            @pl.when(jnp.logical_and(has_next, level_next <= ROW_LEVELS))
            def _():
                arrived(rhs_row, odd_send.at[1])

        @pl.when(chip % 2 == 1)
        def _():
            odd_beneath()
            sent_beneath()
            odd_above()

        @pl.when(chip % 2 == 0)
        def _():
            odd_above()
            sent_above()
            odd_beneath()

        def sent_up(side):
            target = e + (2 * side - 1) * reach
            target_level, _ = place_of(target, levels)
            small = target_level > ROW_LEVELS

            @pl.when(jnp.logical_and(target < slabs, small))
            def _():
                arrived(rhs_state, up_send.at[side])

            @pl.when(jnp.logical_and(target < slabs, jnp.logical_not(small)))
            def _():
                arrived(rhs_row, up_send.at[side])

        def let_go():
            pl.semaphore_signal(go, inc=1, device_id=(s - 1, c), device_id_type=MESH)

        @pl.when(state_role)
        def _():
            let_go()

        pivot_odd[...] = join(times_rows(tall, own_w[PIVOT]))

        pieces = parts // 2

        def convert(index):
            arrived(state_raw.at[index], mat_recv.at[index])
            for part in range(2):
                for k in range(parts):
                    half, place = k // pieces, k % pieces
                    at = (part * pieces + place) * rows
                    high, low = split(state_raw[index, k, part])
                    state_w[index, half, :, at : at + rows] = high
                    state_w[index, half, :, depth + at : depth + at + rows] = low

        def convert_pair(first):
            @pl.loop(first, first + 1 + has_above.astype(jnp.int32))
            def _(index):
                convert(index)

        def by_halves(index, vectors, take):
            tall = split_tall(side_by_side(vectors))
            for half in range(2):
                product = join(times_columns(tall, state_w[index, half]))
                for place in range(pieces):
                    take(half * pieces + place, product[:, place * rows : (place + 1) * rows])
                yield pl.ds(half * pieces, pieces)

        @pl.when(state_role)
        def _():
            @pl.when(not_root)
            def _():
                convert(jnp.where(jnp.logical_and(odd_pair == 0, has_above), ABOVE_R, BENEATH_R))

            arrived(rhs_state, rhs_recv)
            arrived(state_in.at[0, 1, pl.ds(0, parts - 1)], reduce_recv.at[0, 1])
            state_x[...] = rhs_state[...] - state_in[0, 1]

            @pl.when(not_root)
            def _():
                arrived(state_in.at[0, 0], reduce_recv.at[0, 0])
                state_x[...] -= state_in[0, 0]

            @pl.loop(1, level)
            def _(j):
                arrived(state_in.at[j, 1], reduce_recv.at[j, 1])
                state_x[...] -= state_in[j, 1]

                @pl.when(not_root)
                def _():
                    arrived(state_in.at[j, 0], reduce_recv.at[j, 0])
                    state_x[...] -= state_in[j, 0]

            @pl.when(not_root)
            def _():
                @pl.loop(0, 2)
                def _(turn_id):
                    side = jnp.where(odd_pair == 1, turn_id, 1 - turn_id)
                    target = e + (2 * side - 1) * reach

                    @pl.when(target < slabs)
                    def _():
                        @pl.when(jnp.logical_and(turn_id == 1, has_above))
                        def _():
                            convert(side)

                        def put(k, product):
                            state_out[side, k] = product

                        for half in by_halves(side, state_x[...], put):
                            send(
                                state_out.at[side, half],
                                state_in.at[level, 1 - side, half],
                                up_send.at[side],
                                reduce_recv.at[level, 1 - side],
                                (target + 1, c),
                            )

        @pl.when(row_role)
        def _():
            for index in (BENEATH_R, ABOVE_R):
                arrived(row_raw.at[index], mat_recv.at[index])
                row_w[index] = stacked(row_raw[index])
            arrived(rhs_row, rhs_recv)
            arrived(row_in.at[0, 1, pl.ds(0, parts - 1)], reduce_recv.at[0, 1])
            arrived(row_in.at[0, 0], reduce_recv.at[0, 0])
            row_x[...] = rhs_row[...] - row_in[0, 1] - row_in[0, 0]

            for j in range(1, ROW_LEVELS):
                @pl.when(level > j)
                def _():
                    arrived(row_in.at[j, 1], reduce_recv.at[j, 1])
                    arrived(row_in.at[j, 0], reduce_recv.at[j, 0])
                    row_x[...] -= row_in[j, 1] + row_in[j, 0]

            row_tall = split_tall(side_by_side(row_x[...]))

            @pl.loop(0, 2)
            def _(turn_id):
                side = jnp.where(odd_pair == 1, turn_id, 1 - turn_id)
                target = e + (2 * side - 1) * reach

                @pl.when(target < slabs)
                def _():
                    row_out[side] = join(times_rows(row_tall, row_w[side]))
                    target_level, _ = place_of(target, levels)
                    send_rows(
                        row_out.at[side],
                        target + 1,
                        target_level > ROW_LEVELS,
                        level,
                        1 - side,
                        up_send.at[side],
                    )

                @pl.when(turn_id == 0)
                def _():
                    sent_up(side)

            let_go()

        def send_solved(j, side, half):
            target = s + (2 * side - 1) * jnp.left_shift(jnp.int32(1), j)
            send(
                solved.at[half], solve_in.at[1 - side, half], solve_send.at[j, side],
                solve_recv.at[1 - side], (target, c),
            )

        def send_tier(j, half):
            send_solved(j, 1, half)

            @pl.when(not_root)
            def _():
                send_solved(j, 0, half)

        def first_tier(half):
            @pl.when(level > 1)
            def _():
                send_tier(level - 1, half)

        def put_solved(k, product):
            solved[k] = product

        def take_off(k, product):
            solved[k] -= product

        @pl.when(is_root)
        def _():
            convert(PIVOT)
            for half in by_halves(PIVOT, state_x[...], put_solved):
                first_tier(half)

        @pl.when(not_root)
        def _():
            @pl.when(state_role)
            def _():
                around(
                    s,
                    lambda device: send(
                        state_x, row_x.at[:, states_of(c)], gather_send, gather_recv, device
                    ),
                    skip_own=True,
                )
                row_x[:, states_of(c)] = state_x[...]
                arrived(psi_full.at[pl.ds(0, parts - 1)], gather_recv)

            arrived(row_raw.at[PIVOT], mat_recv.at[PIVOT])
            row_w[PIVOT] = stacked(row_raw[PIVOT])
            pivot_rows[...] = join(
                times_rows(split_tall(side_by_side(row_x[...])), row_w[PIVOT])
            )
            around(
                s,
                lambda device: send(
                    pivot_rows.at[states_of(device[1])], solved.at[c], part_send, part_recv, device
                ),
                skip_own=True,
            )
            solved[c] = pivot_rows[states_of(c)]
            convert_pair(BENEATH_S)
            arrived(rhs_state.at[pl.ds(0, parts - 1)], part_recv)

            early = jnp.where(jnp.logical_or(odd_pair == 1, jnp.logical_not(has_above)), 1, 0)
            last = 1 - early

            @pl.when(jnp.logical_or(early == 0, has_above))
            def _():
                arrived(solve_in.at[early], solve_recv.at[early])
                for _ in by_halves(BENEATH_S + early, solve_in[early], take_off):
                    pass

            arrived(solve_in.at[last], solve_recv.at[last])
            for half in by_halves(BENEATH_S + last, solve_in[last], take_off):
                first_tier(half)

        @pl.loop(1, level - 1)
        def _(i):
            send_tier(level - 1 - i, pl.ds(0, parts))

        @pl.when(not_root)
        def _():
            around(
                s - 2,
                lambda device: send(
                    solved, odd_in.at[1, :, states_of(c)], last_send.at[1], last_recv.at[1], device
                ),
            )

        around(
            s,
            lambda device: send(
                solved, odd_in.at[0, :, states_of(c)], last_send.at[0], last_recv.at[0], device
            ),
            skip_own=True,
        )
        odd_in[0, :, states_of(c)] = solved[...]
        around(
            s - 1,
            lambda device: send(
                solved.at[device[1]], out_in.at[states_of(c)], out_send, out_recv, device
            ),
        )

        def settle(side):
            def take():
                if side == 0:
                    arrived(solved_three, last_recv.at[0])
                else:
                    arrived(odd_in.at[1], last_recv.at[1])
                pivot_odd[...] -= join(
                    times_rows(split_tall(side_by_side(odd_in[side])), own_w[BENEATH_S + side])
                )

            if side == 0:
                take()
            else:
                pl.when(has_next)(take)

        solved_three = psi_full.at[pl.ds(0, parts - 1)]

        @pl.when(chip % 2 == 1)
        def _():
            settle(1)
            settle(0)

        @pl.when(chip % 2 == 0)
        def _():
            settle(0)
            settle(1)

        out[0] = pivot_odd[...].T

        arrived(psi_full.at[pl.ds(0, parts - 1)], psi_send)
        arrived(x_full.at[pl.ds(0, parts - 1)], x_send)
        arrived(up_in, serve_send)

        @pl.when(chip % 2 == 1)
        def _():
            sent_above()

        @pl.when(chip % 2 == 0)
        def _():
            sent_beneath()

        @pl.when(has_next)
        def _():
            arrived(tunnel_in, next_send)
            arrived(prev_parts, prev_send)

        @pl.when(not_root)
        def _():
            @pl.loop(0, 2)
            def _(side):
                @pl.when(jnp.logical_or(state_role, side == odd_pair))
                def _():
                    sent_up(side)

            arrived(rhs_row, last_send.at[1])

        arrived(psi_full.at[pl.ds(0, parts - 1)], last_send.at[0])
        arrived(rhs_state, out_send)

        @pl.when(not_root)
        def _():
            arrived(rhs_state.at[pl.ds(0, parts - 1)], part_send)

            @pl.when(state_role)
            def _():
                arrived(psi_full.at[pl.ds(0, parts - 1)], gather_send)

        @pl.loop(1, level)
        def _(j):
            arrived(solved, solve_send.at[j, 1])

            @pl.when(not_root)
            def _():
                arrived(solved, solve_send.at[j, 0])


def per_device(*args):
    slabs = lax.axis_size("slab")
    levels = slabs.bit_length() - 1
    parts = lax.axis_size("col")
    psi = args[0]
    rows, width = psi.shape[1:]
    depth = parts * rows
    quarter = width // parts
    f32, bf16 = jnp.float32, jnp.bfloat16

    def whole(*lead):
        return pltpu.VMEM((*lead, parts, width, rows), f32)

    def piece(*lead):
        return pltpu.VMEM((*lead, parts, quarter, rows), f32)

    dma = pltpu.SemaphoreType.DMA
    return pl.pallas_call(
        functools.partial(kernel, slabs, levels, parts),
        out_shape=jax.ShapeDtypeStruct(psi.shape, psi.dtype),
        in_specs=[pl.BlockSpec(memory_space=pl.ANY)] * len(args),
        out_specs=pl.BlockSpec(memory_space=pltpu.VMEM),
        scratch_shapes=[
            pltpu.VMEM((rows, width), f32),
            pltpu.VMEM((rows, depth), f32),
            pltpu.VMEM((rows, depth), f32),
            pltpu.VMEM((5, 2, rows, depth), f32),
            pltpu.VMEM((5, 2, depth, rows), f32),
            whole(),
            pltpu.VMEM((rows, depth), f32),
            pltpu.VMEM((width, rows), f32),
            pltpu.VMEM((width, rows), f32),
            whole(),
            whole(),
            whole(),
            pltpu.VMEM((2 * rows, depth), bf16),
            pltpu.VMEM((2 * rows, depth), bf16),
            pltpu.VMEM((5, 4 * rows, depth), bf16),
            pltpu.VMEM((3, 2, rows, depth), f32),
            pltpu.VMEM((3, 4 * rows, depth), bf16),
            pltpu.VMEM((5, parts, 2, depth, rows), f32),
            pltpu.VMEM((5, 2, depth, 2 * depth), bf16),
            pltpu.VMEM((width, rows), f32),
            pltpu.VMEM((2, width, rows), f32),
            whole(),
            whole(ROW_LEVELS, 2),
            whole(),
            pltpu.VMEM((2, width, rows), f32),
            piece(),
            piece(levels, 2),
            piece(),
            piece(2),
            piece(2),
            piece(),
            whole(2),
            pltpu.VMEM((width, rows), f32),
            pltpu.VMEM((width, rows), f32),
            dma((8,)),
            *[dma] * 10,
            dma((5,)),
            dma((5,)),
            dma((2,)),
            dma((2,)),
            dma((levels, 2)),
            dma((levels, 2)),
            dma((2,)),
            dma((2,)),
            dma((2,)),
            dma,
            dma,
            *[dma] * 6,
            pltpu.SemaphoreType.REGULAR,
        ],
        compiler_params=pltpu.CompilerParams(
            collective_id=0, has_side_effects=True, vmem_limit_bytes=56 * 2**20
        ),
    )(*args)


def solution(mesh):
    vector = P("slab", "col", None)
    block = P("slab", None, "col", None)
    return jax.shard_map(
        per_device,
        mesh=mesh,
        in_specs=(vector,) * 3 + (block,) * 5,
        out_specs=vector,
        check_vma=False,
    )
```
